128 devices in a mesh: wide: 16 (over x_lo, y, core), narrow: 8 (over z, x_hi).
Axes of the slice: x: 4 (x_hi: 2, x_lo: 2; x = x_hi * 2 + x_lo), y: 4, z: 4, core: 2. Of those that a mesh axis runs over, the one named last changes fastest.
Arguments:
- clip_tokens: bfloat16 [256, 256, 1152], P(('wide', 'narrow')), may hold values from -6 to 6
- cotangent: bfloat16 [256, 256, 1152], P(None, ('wide', 'narrow')), may hold values from -24 to 24
- qkv_spatial: bfloat16 [1152, 1728], replicated, may hold values from -0.1875 to 0.1875
- proj_spatial: bfloat16 [1152, 576], replicated, may hold values from -0.25 to 0.25
- adaln_spatial: float32 [3, 1152], replicated, may hold values from -4 to 4
- qknorm_spatial: float32 [2, 72], replicated, may hold values from 0.5 to 2.5
- qkv_temporal: bfloat16 [1152, 1728], replicated, may hold values from -0.1875 to 0.1875
- proj_temporal: bfloat16 [1152, 576], replicated, may hold values from -0.25 to 0.25
- adaln_temporal: float32 [3, 1152], replicated, may hold values from -4 to 4
- qknorm_temporal: float32 [2, 72], replicated, may hold values from 0.5 to 2.5
Outputs:
- result: bfloat16 [256, 256, 1152], P(None, ('wide', 'narrow'))
- grad_clip: bfloat16 [256, 256, 1152], P(('wide', 'narrow'))
- grad_qkv_spatial: float32 [1152, 1728], P(('wide', 'narrow'))
- grad_proj_spatial: float32 [1152, 576], P(('wide', 'narrow'))
- grad_qkv_temporal: float32 [1152, 1728], P(('wide', 'narrow'))
- grad_proj_temporal: float32 [1152, 576], P(('wide', 'narrow'))
The draws below stay inside these ranges and needn't reach their ends.
All inputs are finite; a program needn't handle non-finite values.
Results may differ from the reference program's by a relative error of at most 0.015.
The reference program's roundings to bfloat16 on the way count: a program that leaves them out, or rounds other values in their place, can miss the bound.
Values may be sent and summed in bfloat16 or wider, within the bound.
A program may use at most 192 MiB of HBM per device.

```python
import math
import jax
import jax.numpy as jnp
from jax import lax

D = 1152
HDIM = 72
HEADS = 8
HD = 576
P_SIZE = 256
FRAMES = 256


def spiked(values, stream_key, source, target, shards_of, factor):
    owner, partner = [(jnp.arange(values.shape[axis_at]) // (values.shape[axis_at] // shards_of)).reshape([-1 if axis == axis_at else 1 for axis in range(values.ndim)]) for axis_at in (source, target)]
    chosen = jax.random.permutation(stream_key, shards_of)[partner]
    strong = (owner == chosen) | (owner == (partner + shards_of // 2) % shards_of)
    return jnp.where(strong, factor * values, values)


def block_scale(own_key, shape, shards, low, high):
    level, own = 1.0, jax.random.fold_in(own_key, 6)
    for position, shards_of in shards:
        heights = jnp.exp(jax.random.uniform(jax.random.fold_in(own, position), (shards_of,), jnp.float32, low / len(shards), high / len(shards)))
        level = level * jnp.repeat(heights, shape[position] // shards_of).reshape([-1 if axis == position else 1 for axis in range(len(shape))])
    return level


def bell_draw(rng, shape, deviation, limit, shards=(), kind=jnp.bfloat16):
    entries = deviation * jax.random.normal(rng, shape, jnp.float32)
    if shards:
        entries = entries * block_scale(rng, shape, shards, -0.22, 0.18)
    return jnp.clip(entries, -limit, limit).astype(kind)


def bell_draw_with(rng, dims, deviation, most, cuts, heavy, kind=jnp.bfloat16):
    values = deviation * jax.random.normal(rng, dims, jnp.float32)
    if cuts:
        values = values * block_scale(rng, dims, cuts, -0.22, 0.18)
    return jnp.clip(spiked(values, jax.random.fold_in(rng, 3), *heavy), -most, most).astype(kind)


def setup_inputs(seed: int = 0) -> dict:
    streams_of = jax.random.split(jax.random.key(seed), 11)
    return {
        "clip_tokens": bell_draw(streams_of[0], (FRAMES, P_SIZE, D), 1.0, 6.0, ((0, 128),)),
        "cotangent": bell_draw_with(streams_of[1], (FRAMES, P_SIZE, D), 1.0, 24.0, ((1, 128),), (1, 2, 128, 5.5)),
        "qkv_spatial": bell_draw(streams_of[2], (D, 3 * HD), D ** -0.5, 0.1875),
        "proj_spatial": bell_draw(streams_of[3], (D, HD), HD ** -0.5, 0.25),
        "adaln_spatial": bell_draw(streams_of[4], (3, D), 1.0, 4.0, (), jnp.float32),
        "qknorm_spatial": jnp.clip(jnp.exp(jax.random.uniform(streams_of[5], (2, HDIM), jnp.float32, math.log(0.5), math.log(2.5))), 0.5, 2.5),
        "qkv_temporal": bell_draw(streams_of[6], (D, 3 * HD), D ** -0.5, 0.1875),
        "proj_temporal": bell_draw(streams_of[7], (D, HD), HD ** -0.5, 0.25),
        "adaln_temporal": bell_draw(streams_of[8], (3, D), 1.0, 4.0, (), jnp.float32),
        "qknorm_temporal": jnp.clip(jnp.exp(jax.random.uniform(streams_of[9], (2, HDIM), jnp.float32, math.log(0.5), math.log(2.5))), 0.5, 2.5),
    }


epsilon = 1e-06

def modulate(inputs, modulation):
    values = inputs.astype(jnp.float32)
    centre = values - lax.optimization_barrier(jnp.mean(values, axis=-1, keepdims=True))
    spread = lax.optimization_barrier(jnp.mean(centre * centre, axis=-1, keepdims=True))
    return centre * lax.rsqrt(spread + epsilon) * (1.0 + modulation[1]) + modulation[0]

def rms_scale(vectors, gain):
    return vectors * lax.rsqrt(lax.optimization_barrier(jnp.mean(vectors * vectors, axis=-1, keepdims=True)) + epsilon) * gain

def attend(qkv, norm_gain, seq_first):
    lead, second, _ = qkv.shape
    pieces = qkv.reshape(lead, second, 3, HEADS, HDIM)
    queries = rms_scale(pieces[:, :, 0], norm_gain[0])
    keys_all = rms_scale(pieces[:, :, 1], norm_gain[1])
    values = pieces[:, :, 2]
    if seq_first:
        score_form, mix_form = ('lbhd,mbhd->bhlm', 'bhlm,mbhd->lbhd')
    else:
        score_form, mix_form = ('blhd,bmhd->bhlm', 'bhlm,bmhd->blhd')
    scores = jnp.einsum(score_form, queries, keys_all, precision=lax.Precision.HIGHEST) / jnp.sqrt(jnp.float32(HDIM))
    weights = jnp.exp(scores)
    weights = weights / lax.optimization_barrier(jnp.sum(weights, axis=-1, keepdims=True))
    mixed = jnp.einsum(mix_form, weights, values, precision=lax.Precision.HIGHEST)
    return mixed.reshape(lead, second, HEADS * HDIM)

def block_forward(inputs, qkv_weight, proj_weight, modulation, norm_gain, seq_first):
    lead, second, features = inputs.shape
    normed = modulate(inputs, modulation).astype(jnp.bfloat16)
    qkv = jnp.dot(normed.reshape(lead * second, features), qkv_weight, preferred_element_type=jnp.float32)
    qkv = qkv.reshape(lead, second, qkv_weight.shape[1])
    mixed, pull_back = jax.vjp(lambda inner: attend(inner, norm_gain, seq_first), qkv)
    mixed_low = mixed.astype(jnp.bfloat16)
    projected = lax.dot_general(mixed_low.reshape(lead * second, -1), proj_weight, (((1,), (1,)), ((), ())), preferred_element_type=jnp.float32)
    output = inputs.astype(jnp.float32) + modulation[2] * projected.reshape(lead, second, features)
    return (output.astype(jnp.bfloat16), (normed, mixed_low, pull_back))

def block_backward(inputs, cotangent, qkv_weight, proj_weight, modulation, stored):
    normed, mixed_low, pull_back = stored
    lead, second, features = inputs.shape
    rows = lead * second
    branch = (modulation[2] * cotangent.astype(jnp.float32)).astype(jnp.bfloat16).reshape(rows, features)
    grad_proj = lax.dot_general(branch, mixed_low.reshape(rows, -1), (((0,), (0,)), ((), ())), preferred_element_type=jnp.float32)
    grad_mixed = jnp.dot(branch, proj_weight, preferred_element_type=jnp.float32).reshape(lead, second, -1)
    grad_qkv = pull_back(grad_mixed)[0].astype(jnp.bfloat16).reshape(rows, -1)
    grad_weight = lax.dot_general(normed.reshape(rows, features), grad_qkv, (((0,), (0,)), ((), ())), preferred_element_type=jnp.float32)
    grad_normed = lax.dot_general(grad_qkv, qkv_weight, (((1,), (1,)), ((), ())), preferred_element_type=jnp.float32)
    norm_pull = jax.vjp(lambda inner: modulate(inner, modulation), inputs.astype(jnp.float32))[1]
    grad_inputs = cotangent.astype(jnp.float32) + norm_pull(grad_normed.reshape(lead, second, features))[0]
    return (grad_inputs, grad_weight, grad_proj)

def reference(clip_tokens, cotangent, qkv_spatial, proj_spatial, adaln_spatial, qknorm_spatial, qkv_temporal, proj_temporal, adaln_temporal, qknorm_temporal):
    frames, patches, features = clip_tokens.shape
    block_size = 8
    clip_blocks = clip_tokens.reshape(frames // block_size, block_size, patches, features)

    def spatial_only(block_rows):
        return block_forward(block_rows, qkv_spatial, proj_spatial, adaln_spatial, qknorm_spatial, False)[0]
    middle = lax.map(spatial_only, clip_blocks).reshape(frames, patches, features)
    turned = jnp.transpose(middle, (1, 0, 2)).reshape(patches // block_size, block_size, frames, features)
    cot_turned = jnp.transpose(cotangent, (1, 0, 2)).reshape(patches // block_size, block_size, frames, features)
    empty = (jnp.zeros(qkv_temporal.shape, jnp.float32), jnp.zeros(proj_temporal.shape, jnp.float32))

    def temporal_step(totals, block_pair):
        block_rows, block_cot = block_pair
        output, stored = block_forward(block_rows, qkv_temporal, proj_temporal, adaln_temporal, qknorm_temporal, False)
        grad_rows, grad_weight, grad_proj = block_backward(block_rows, block_cot, qkv_temporal, proj_temporal, adaln_temporal, stored)
        return ((totals[0] + grad_weight, totals[1] + grad_proj), (output, grad_rows.astype(jnp.bfloat16)))
    temporal_totals, (outputs, grad_turned) = lax.scan(temporal_step, empty, (turned, cot_turned))
    result = jnp.transpose(outputs.reshape(patches, frames, features), (1, 0, 2))
    grad_middle = jnp.transpose(grad_turned.reshape(patches, frames, features), (1, 0, 2))
    grad_blocks = grad_middle.reshape(frames // block_size, block_size, patches, features)

    def spatial_step(totals, block_pair):
        block_rows, block_cot = block_pair
        stored = block_forward(block_rows, qkv_spatial, proj_spatial, adaln_spatial, qknorm_spatial, False)[1]
        grad_rows, grad_weight, grad_proj = block_backward(block_rows, block_cot, qkv_spatial, proj_spatial, adaln_spatial, stored)
        return ((totals[0] + grad_weight, totals[1] + grad_proj), grad_rows.astype(jnp.bfloat16))
    spatial_totals, grad_rows = lax.scan(spatial_step, (jnp.zeros(qkv_spatial.shape, jnp.float32), jnp.zeros(proj_spatial.shape, jnp.float32)), (clip_blocks, grad_blocks))
    grad_clip = grad_rows.reshape(frames, patches, features)
    factor = 1.0 / jnp.sqrt(jnp.float32(frames * patches))
    return (result, grad_clip, spatial_totals[0] * factor, spatial_totals[1] * factor, temporal_totals[0] * factor, temporal_totals[1] * factor)
```

```python
import functools
import math

import jax
import jax.numpy as jnp
from jax import lax
from jax.experimental import pallas as pl
from jax.experimental.pallas import tpu as pltpu
from jax.sharding import PartitionSpec as P

HDIM = 72
HEADS = 8


epsilon = 1e-06


def modulate(inputs, modulation):
    values = inputs.astype(jnp.float32)
    centre = values - jnp.mean(values, axis=-1, keepdims=True)
    spread = jnp.mean(centre * centre, axis=-1, keepdims=True)
    return centre * lax.rsqrt(spread + epsilon) * (1.0 + modulation[1]) + modulation[0]


def rms_scale(vectors, gain):
    return vectors * lax.rsqrt(jnp.mean(vectors * vectors, axis=-1, keepdims=True) + epsilon) * gain


def attend(qkv, norm_gain, seq_first):
    lead, second, _ = qkv.shape
    pieces = qkv.reshape(lead, second, 3, HEADS, HDIM)
    queries = rms_scale(pieces[:, :, 0], norm_gain[0])
    keys_all = rms_scale(pieces[:, :, 1], norm_gain[1])
    values = pieces[:, :, 2]
    if seq_first:
        score_form, mix_form = ("lbhd,mbhd->bhlm", "bhlm,mbhd->lbhd")
    else:
        score_form, mix_form = ("blhd,bmhd->bhlm", "bhlm,bmhd->blhd")
    scores = jnp.einsum(score_form, queries, keys_all, precision=lax.Precision.HIGHEST) / jnp.sqrt(
        jnp.float32(HDIM)
    )
    weights = jnp.exp(scores)
    weights = weights / jnp.sum(weights, axis=-1, keepdims=True)
    mixed = jnp.einsum(mix_form, weights, values, precision=lax.Precision.HIGHEST)
    return mixed.reshape(lead, second, HEADS * HDIM)


def block_forward(inputs, qkv_weight, proj_weight, modulation, norm_gain, seq_first):
    lead, second, features = inputs.shape
    normed = modulate(inputs, modulation).astype(jnp.bfloat16)
    qkv = jnp.dot(
        normed.reshape(lead * second, features), qkv_weight, preferred_element_type=jnp.float32
    )
    qkv = qkv.reshape(lead, second, qkv_weight.shape[1])
    mixed, pull_back = jax.vjp(lambda inner: attend(inner, norm_gain, seq_first), qkv)
    mixed_low = mixed.astype(jnp.bfloat16)
    projected = lax.dot_general(
        mixed_low.reshape(lead * second, -1),
        proj_weight,
        (((1,), (1,)), ((), ())),
        preferred_element_type=jnp.float32,
    )
    output = inputs.astype(jnp.float32) + modulation[2] * projected.reshape(lead, second, features)
    return (output.astype(jnp.bfloat16), (normed, mixed_low, pull_back))


def block_backward(inputs, cotangent, qkv_weight, proj_weight, modulation, stored):
    normed, mixed_low, pull_back = stored
    lead, second, features = inputs.shape
    rows = lead * second
    branch = (
        (modulation[2] * cotangent.astype(jnp.float32)).astype(jnp.bfloat16).reshape(rows, features)
    )
    grad_proj = lax.dot_general(
        branch,
        mixed_low.reshape(rows, -1),
        (((0,), (0,)), ((), ())),
        preferred_element_type=jnp.float32,
    )
    grad_mixed = jnp.dot(branch, proj_weight, preferred_element_type=jnp.float32).reshape(
        lead, second, -1
    )
    grad_qkv = pull_back(grad_mixed)[0].astype(jnp.bfloat16).reshape(rows, -1)
    grad_weight = lax.dot_general(
        normed.reshape(rows, features),
        grad_qkv,
        (((0,), (0,)), ((), ())),
        preferred_element_type=jnp.float32,
    )
    grad_normed = lax.dot_general(
        grad_qkv, qkv_weight, (((1,), (1,)), ((), ())), preferred_element_type=jnp.float32
    )
    norm_pull = jax.vjp(lambda inner: modulate(inner, modulation), inputs.astype(jnp.float32))[1]
    grad_inputs = (
        cotangent.astype(jnp.float32) + norm_pull(grad_normed.reshape(lead, second, features))[0]
    )
    return (grad_inputs, grad_weight, grad_proj)


def to_columns(middle):
    return lax.all_to_all(middle, ("wide", "narrow"), split_axis=1, concat_axis=0, tiled=True)


def to_frames(gradient):
    return lax.all_to_all(gradient, ("wide", "narrow"), split_axis=0, concat_axis=1, tiled=True)


MESH = pl.DeviceIdType.MESH
LANES = 128
PART_ROWS = 112
PARTS = 3
SLAB_ROWS = PART_ROWS * PARTS
AXIS_ORDER = (("y", "z", "x"), ("z", "x", "y"), ("x", "y", "z"))


def place():
    wide = lax.axis_index("wide")
    narrow = lax.axis_index("narrow")
    x_lo, y, core = wide // 8, (wide // 2) % 4, wide % 2
    z, x_hi = narrow // 2, narrow % 2
    return {"x": x_hi * 2 + x_lo, "y": y, "z": z, "core": core}


def device_of(at):
    wide = (at["x"] % 2) * 8 + at["y"] * 2 + at["core"]
    narrow = at["z"] * 2 + at["x"] // 2
    return (wide, narrow)


def moved(at, axis, step):
    size = 2 if axis == "core" else 4
    return {**at, axis: (at[axis] + step) % size}


def add_rows(count, target, sources, cast):
    def step(index, carry):
        total = sources[0](index).astype(jnp.float32)
        for source in sources[1:]:
            total = total + source(index).astype(jnp.float32)
        target(index, total.astype(cast))
        return carry

    lax.fori_loop(0, count, step, 0)


def scatter_kernel(scale, slabs, out, own, from_core, first, second, third, recv1, recv2, recv3,
                   own_sem, core_send, core_recv, send_sem, recv_sem):
    at = place()
    partner = device_of(moved(at, "core", 1))
    core = at["core"]
    barrier = pltpu.get_barrier_semaphore()
    peers = [partner] + [device_of(moved(at, a, d)) for a in ("x", "y", "z") for d in (1, 3)]
    for peer in peers:
        pl.semaphore_signal(barrier, inc=1, device_id=peer, device_id_type=MESH)
    pl.semaphore_wait(barrier, len(peers))

    core_copies, own_copies = [], []
    for part in range(PARTS):
        rows = pl.ds(part * PART_ROWS, PART_ROWS)
        copy = pltpu.make_async_remote_copy(
            src_ref=slabs.at[:, :, 1 - core, :, :, rows],
            dst_ref=from_core.at[part],
            send_sem=core_send.at[part], recv_sem=core_recv.at[part],
            device_id=partner, device_id_type=MESH)
        copy.start()
        core_copies.append(copy)
        mine = pltpu.make_async_copy(slabs.at[:, :, core, :, :, rows], own.at[part], own_sem.at[part])
        mine.start()
        own_copies.append(mine)

    bufs = (first, second, third)
    recvs = (recv1, recv2, recv3)

    def halves(level, block):
        if level == 0:
            return block.at[0:2], block.at[2:4]
        if level == 1:
            return block.at[0:2], block.at[2:4]
        return block.at[0:64], block.at[64:PART_ROWS]

    pending = {}

    def copy_of(part, level, direction, kind, src, dst):
        step = 1 if direction == 0 else 3
        axis = AXIS_ORDER[part][level]
        slot = ((part * 3 + level) * 2 + direction) * 3 + kind
        copy = pltpu.make_async_remote_copy(
            src_ref=src, dst_ref=dst,
            send_sem=send_sem.at[slot], recv_sem=recv_sem.at[slot],
            device_id=device_of(moved(at, axis, step)), device_id_type=MESH)
        copy.start()
        pending[(part, level, direction, kind)] = copy

    def start_level(part, level):
        axis = AXIS_ORDER[part][level]
        here = at[axis]
        source = bufs[level].at[part]
        recv = recvs[level].at[part]
        for direction in (0, 1):
            relay_half, plain_half = direction, 1 - direction
            far = source.at[(here + 2) % 4]
            near = source.at[(here + (1 if direction == 0 else 3)) % 4]
            copy_of(part, level, direction, 0, halves(level, far)[relay_half],
                    halves(level, recv.at[direction, 0])[relay_half])
            copy_of(part, level, direction, 1, halves(level, near)[plain_half],
                    halves(level, recv.at[direction, 1])[plain_half])

    def relay_level(part, level):
        axis = AXIS_ORDER[part][level]
        here = at[axis]
        source = bufs[level].at[part]
        recv = recvs[level].at[part]
        for direction in (0, 1):
            pending[(part, level, direction, 0)].wait_recv()
            near = halves(level, source.at[(here + (1 if direction == 0 else 3)) % 4])[direction]
            came = halves(level, recv.at[direction, 0])[direction]
            if level == 0:
                def target(i, v):
                    came[i // 4, i % 4] = v
                add_rows(8, target, [lambda i: came[i // 4, i % 4], lambda i: near[i // 4, i % 4]], jnp.bfloat16)
            elif level == 1:
                def target(i, v):
                    came[i] = v
                add_rows(2, target, [lambda i: came[i], lambda i: near[i]], jnp.bfloat16)
            else:
                came[...] = (came[...].astype(jnp.float32) + near[...].astype(jnp.float32)).astype(jnp.bfloat16)
            copy_of(part, level, direction, 2, came, halves(level, recv.at[direction, 1])[direction])

    def finish_level(part, level):
        axis = AXIS_ORDER[part][level]
        here = at[axis]
        source = bufs[level].at[part].at[here]
        recv = recvs[level].at[part]
        for direction in (0, 1):
            pending[(part, level, direction, 1)].wait_recv()
            pending[(part, level, direction, 2)].wait_recv()
        plus, minus = recv.at[0, 1], recv.at[1, 1]
        if level == 0:
            goal = second.at[part]

            def target(i, v):
                goal[i // 4, i % 4] = v
            add_rows(16, target, [lambda i: source[i // 4, i % 4], lambda i: plus[i // 4, i % 4],
                                  lambda i: minus[i // 4, i % 4]], jnp.bfloat16)
        elif level == 1:
            goal = third.at[part]

            def target(i, v):
                goal[i] = v
            add_rows(4, target, [lambda i: source[i], lambda i: plus[i], lambda i: minus[i]], jnp.bfloat16)
        else:
            out[pl.ds(part * PART_ROWS, PART_ROWS), :] = (
                source[...].astype(jnp.float32) + plus[...].astype(jnp.float32)
                + minus[...].astype(jnp.float32)) * scale

    for part in range(PARTS):
        core_copies[part].wait_recv()
        own_copies[part].wait()
        order = AXIS_ORDER[part]

        def target(index, value):
            digit = {"x": (index % 2) * 2 + index // 32, "y": (index // 8) % 4, "z": (index // 2) % 4}
            first[part, digit[order[0]], digit[order[1]], digit[order[2]]] = value

        mine, theirs = own.at[part], from_core.at[part]
        add_rows(64, target,
                 [lambda i: mine[i // 32, (i // 8) % 4, (i // 2) % 4, i % 2],
                  lambda i: theirs[i // 32, (i // 8) % 4, (i // 2) % 4, i % 2]], jnp.bfloat16)
        start_level(part, 0)
    for level in range(3):
        for part in range(PARTS):
            relay_level(part, level)
        for part in range(PARTS):
            finish_level(part, level)
            if level < 2:
                start_level(part, level + 1)
    for copy in core_copies:
        copy.wait_send()
    for copy in pending.values():
        copy.wait_send()


def scatter_sums(slabs, scale):
    slabs = slabs.reshape(2, 4, 2, 4, 2, SLAB_ROWS, LANES)
    bf = jnp.bfloat16
    return pl.pallas_call(
        functools.partial(scatter_kernel, scale),
        out_shape=jax.ShapeDtypeStruct((SLAB_ROWS, LANES), jnp.float32),
        in_specs=[pl.BlockSpec(memory_space=pl.ANY)],
        out_specs=pl.BlockSpec(memory_space=pltpu.VMEM),
        scratch_shapes=[
            pltpu.VMEM((PARTS, 2, 4, 4, 2, PART_ROWS, LANES), bf),
            pltpu.VMEM((PARTS, 2, 4, 4, 2, PART_ROWS, LANES), bf),
            pltpu.VMEM((PARTS, 4, 4, 4, PART_ROWS, LANES), bf),
            pltpu.VMEM((PARTS, 4, 4, PART_ROWS, LANES), bf),
            pltpu.VMEM((PARTS, 4, PART_ROWS, LANES), bf),
            pltpu.VMEM((PARTS, 2, 2, 4, 4, PART_ROWS, LANES), bf),
            pltpu.VMEM((PARTS, 2, 2, 4, PART_ROWS, LANES), bf),
            pltpu.VMEM((PARTS, 2, 2, PART_ROWS, LANES), bf),
            pltpu.SemaphoreType.DMA((PARTS,)),
            pltpu.SemaphoreType.DMA((PARTS,)),
            pltpu.SemaphoreType.DMA((PARTS,)),
            pltpu.SemaphoreType.DMA((PARTS * 18,)),
            pltpu.SemaphoreType.DMA((PARTS * 18,)),
        ],
        compiler_params=pltpu.CompilerParams(
            collective_id=0, has_side_effects=True, vmem_limit_bytes=60 << 20),
        name="scatter_sums",
    )(slabs)


def reduce_grads(first, second, third, fourth, scale):
    shards, per = 128, first.shape[0] // 128
    wide, slim = first.shape[1], second.shape[1]
    whole = jnp.concatenate([first, second, third, fourth], axis=1)
    slabs = whole.astype(jnp.bfloat16).reshape(shards, -1, LANES)
    used = slabs.shape[1]
    slabs = jnp.pad(slabs, ((0, 0), (0, SLAB_ROWS - used), (0, 0)))
    summed = scatter_sums(slabs, scale)[:used].reshape(per, 2 * (wide + slim))
    cuts = (wide, wide + slim, 2 * wide + slim)
    return tuple(jnp.split(summed, cuts, axis=1))


def body(
    clip_tokens,
    cotangent,
    qkv_spatial,
    proj_spatial,
    adaln_spatial,
    qknorm_spatial,
    qkv_temporal,
    proj_temporal,
    adaln_temporal,
    qknorm_temporal,
):
    middle, stored_spatial = block_forward(
        clip_tokens, qkv_spatial, proj_spatial, adaln_spatial, qknorm_spatial, False
    )
    turned = to_columns(middle)
    result, stored_temporal = block_forward(
        turned, qkv_temporal, proj_temporal, adaln_temporal, qknorm_temporal, True
    )
    grad_turned, grad_qkv_t, grad_proj_t = block_backward(
        turned, cotangent, qkv_temporal, proj_temporal, adaln_temporal, stored_temporal
    )
    grad_middle = to_frames(grad_turned.astype(jnp.bfloat16))
    grad_inputs, grad_qkv_s, grad_proj_s = block_backward(
        clip_tokens, grad_middle, qkv_spatial, proj_spatial, adaln_spatial, stored_spatial
    )
    factor = 1.0 / math.sqrt(turned.shape[0] * clip_tokens.shape[1])
    summed = reduce_grads(grad_qkv_s, grad_proj_s, grad_qkv_t, grad_proj_t, factor)
    return (
        result,
        grad_inputs.astype(jnp.bfloat16),
        summed[0],
        summed[1],
        summed[2],
        summed[3],
    )


def solution(mesh):
    in_specs = (
        P(("wide", "narrow"), None, None),
        P(None, ("wide", "narrow"), None),
        P(),
        P(),
        P(),
        P(),
        P(),
        P(),
        P(),
        P(),
    )
    out_specs = (
        P(None, ("wide", "narrow"), None),
        P(("wide", "narrow"), None, None),
        P(("wide", "narrow"), None),
        P(("wide", "narrow"), None),
        P(("wide", "narrow"), None),
        P(("wide", "narrow"), None),
    )
    return jax.shard_map(body, mesh=mesh, in_specs=in_specs, out_specs=out_specs, check_vma=False)
```

```python
import functools
import math

import jax
import jax.numpy as jnp
from jax import lax
from jax.experimental import pallas as pl
from jax.experimental.pallas import tpu as pltpu
from jax.sharding import PartitionSpec as P

HDIM = 72
HEADS = 8
HD = HDIM * HEADS
MODEL = 1152
TOKENS = 512
SEQ = 256
EPSILON = 1e-06
QKV_TILES, PROJ_TILES = 14, 5
TILES = QKV_TILES + PROJ_TILES
SHARDS = 128
SLAB = 176
NT = (((1,), (1,)), ((), ()))
TN = (((0,), (0,)), ((), ()))
F32, BF16 = jnp.float32, jnp.bfloat16


def centred(x):
    centre = x - jnp.mean(x, axis=-1, keepdims=True)
    spread = jnp.mean(centre * centre, axis=-1, keepdims=True)
    scale = lax.rsqrt(spread + EPSILON)
    return centre * scale, scale


def row_loop(total, step, body, unroll=1):
    lax.fori_loop(0, total // step, lambda i, c: (body(pl.ds(pl.multiple_of(i * step, step), step)), c)[1], 0,
                  unroll=unroll)


def norm_tokens(x_ref, adaln, normed):
    def body(rows):
        hat, _ = centred(x_ref[rows, :].astype(F32))
        normed[rows, :] = (hat * (1.0 + adaln[1:2, :]) + adaln[0:1, :]).astype(BF16)

    row_loop(TOKENS, 16, body, 4)


def project_qkv(normed, weight, qkv_t):
    for start, size in ((0, 512), (512, 512), (1024, 512), (1536, 192)):
        part = jnp.dot(normed[...], weight[:, start:start + size], preferred_element_type=F32)
        qkv_t[start:start + size, :] = part.T


def split3(value):
    high = value.astype(BF16).astype(F32)
    return high, value - high


def heads_loop(qkv_t, gains, mixed_t, dmixed_t, dqkv_t):
    root = 1.0 / math.sqrt(HDIM)

    def body(index, carry):
        head, seq = index // 2, index % 2
        lanes = pl.ds(pl.multiple_of(seq * SEQ, SEQ), SEQ)
        at = [pl.ds(pl.multiple_of(part * HD + head * HDIM, 8), HDIM) for part in range(3)]
        q, k, v = (qkv_t[rows, lanes] for rows in at)
        q_gain, k_gain = gains[:, 0:1], gains[:, 1:2]
        q_scale = lax.rsqrt(jnp.mean(q * q, axis=0, keepdims=True) + EPSILON)
        k_scale = lax.rsqrt(jnp.mean(k * k, axis=0, keepdims=True) + EPSILON)
        q_hat, k_hat = q * q_scale, k * k_scale
        qs, kn = q_hat * (q_gain * root), k_hat * k_gain
        q_high, q_low = split3(qs)
        k_high, k_low = split3(kn)
        q3 = jnp.concatenate([q_high, q_low, q_high], axis=0).astype(BF16)
        k3 = jnp.concatenate([k_high, k_high, k_low], axis=0).astype(BF16)
        raised = jnp.exp(lax.dot_general(k3, q3, TN, preferred_element_type=F32))
        inverse = 1.0 / jnp.sum(raised, axis=0, keepdims=True)
        v_low = v.astype(BF16)
        if mixed_t is not None:
            out = jnp.dot(v_low, raised.astype(BF16), preferred_element_type=F32) * inverse
            mixed_t[at[0], lanes] = out
        if dqkv_t is not None:
            weights = raised * inverse
            d_out = dmixed_t[at[0], lanes].astype(BF16)
            d_weights = lax.dot_general(v_low, d_out, TN, preferred_element_type=F32)
            shift = jnp.sum(weights * d_weights, axis=0, keepdims=True)
            d_scores = (weights * (d_weights - shift)).astype(BF16)
            dv = lax.dot_general(d_out, weights.astype(BF16), NT, preferred_element_type=F32)
            dq = jnp.dot(k_high.astype(BF16), d_scores, preferred_element_type=F32)
            dk = lax.dot_general(q_high.astype(BF16), d_scores, NT, preferred_element_type=F32)
            dq = dq * (q_gain * root)
            dk = dk * k_gain
            dqkv_t[at[0], lanes] = q_scale * (dq - q_hat * jnp.mean(q_hat * dq, axis=0, keepdims=True))
            dqkv_t[at[1], lanes] = k_scale * (dk - k_hat * jnp.mean(k_hat * dk, axis=0, keepdims=True))
            dqkv_t[at[2], lanes] = dv
        return carry

    lax.fori_loop(0, 2 * HEADS, body, 0, unroll=2)


def add_projection(x_ref, mixed, proj, adaln, out_ref):
    def body(rows):
        projected = lax.dot_general(mixed[rows, :HD], proj[...], NT, preferred_element_type=F32)
        out_ref[rows, :] = (x_ref[rows, :].astype(F32) + adaln[2:3, :] * projected).astype(BF16)

    row_loop(TOKENS, 256, body)


def gate_cotangent(cot_ref, adaln, branch):
    def body(rows):
        branch[rows, :] = (adaln[2:3, :] * cot_ref[rows, :].astype(F32)).astype(BF16)

    row_loop(TOKENS, 64, body)


def pull_norm(x_ref, cot_ref, dqkv, weight, adaln, d_normed, out_ref):
    for start in range(0, MODEL, 384):
        d_normed[:, start:start + 384] = lax.dot_general(
            dqkv[:, :3 * HD], weight[start:start + 384, :], NT, preferred_element_type=F32)

    def body(rows):
        hat, scale = centred(x_ref[rows, :].astype(F32))
        u = d_normed[rows, :] * (1.0 + adaln[1:2, :])
        d_x = scale * (u - jnp.mean(u, axis=-1, keepdims=True) - hat * jnp.mean(u * hat, axis=-1, keepdims=True))
        out_ref[rows, :] = (cot_ref[rows, :].astype(F32) + d_x).astype(BF16)

    row_loop(TOKENS, 16, body, 4)


def gradient_slabs(normed, branch, dqkv, mixed, slabs, left, tiles):
    def pair(right, first, lane):
        out = jnp.dot(left[...], right[:, pl.ds(pl.multiple_of(lane, 256), 256)], preferred_element_type=F32)
        tiles[pl.ds(pl.multiple_of(first * MODEL, MODEL), MODEL), :] = out[:, :128]
        tiles[pl.ds(pl.multiple_of(first * MODEL + MODEL, MODEL), MODEL), :] = out[:, 128:]

    left[...] = normed[...].T
    lax.fori_loop(0, QKV_TILES // 2, lambda i, c: (pair(dqkv, 2 * i, 256 * i), c)[1], 0)
    left[...] = branch[...].T
    lax.fori_loop(0, PROJ_TILES // 2, lambda i, c: (pair(mixed, QKV_TILES + 2 * i, 256 * i), c)[1], 0)
    tiles[18 * MODEL:19 * MODEL, :] = jnp.dot(left[...], mixed[:, 512:640], preferred_element_type=F32)

    def gather(s, carry):
        parts = [tiles[pl.ds(tile * MODEL + 9 * s, 8), :] for tile in range(TILES)]
        parts += [tiles[pl.ds(8 * group * MODEL + 9 * s + 8, 8, stride=MODEL), :] for group in range(2)]
        parts.append(tiles[pl.ds(11 * MODEL + 9 * s + 8, 8, stride=MODEL), :])
        for tile in range(0, TILES + 3, 2):
            slabs[s, tile * 8:tile * 8 + 16, :] = jnp.concatenate(parts[tile:tile + 2], axis=0).astype(BF16)
        return carry

    lax.fori_loop(0, SHARDS, gather, 0, unroll=2)


def wide_rows(ref, used, value):
    ref[:, :used] = value.T.astype(BF16)
    ref[:, used:] = jnp.zeros((TOKENS, ref.shape[1] - used), BF16)


def spatial_forward(x, weight, proj, adaln, gains, middle, qkv_t, mixed, normed, mixed_t):
    norm_tokens(x, adaln, normed)
    project_qkv(normed, weight, qkv_t)
    heads_loop(qkv_t, gains, mixed_t, None, None)
    wide_rows(mixed, HD, mixed_t[...])
    add_projection(x, mixed, proj, adaln, middle)


def backward_rest(x, cot, weight, adaln, normed, branch, mixed, dqkv_t, d_x, slabs, dqkv, d_normed, left, tiles):
    wide_rows(dqkv, 3 * HD, dqkv_t[...])
    pull_norm(x, cot, dqkv, weight, adaln, d_normed, d_x)
    gradient_slabs(normed, branch, dqkv, mixed, slabs, left, tiles)


def temporal_both(x, cot, weight, proj, adaln, gains, result, d_x, slabs,
                  normed, qkv_t, mixed_t, mixed, branch, dmixed_t, dqkv_t, *rest):
    norm_tokens(x, adaln, normed)
    project_qkv(normed, weight, qkv_t)
    gate_cotangent(cot, adaln, branch)
    dmixed_t[...] = jnp.dot(branch[...], proj[...], preferred_element_type=F32).T
    heads_loop(qkv_t, gains, mixed_t, dmixed_t, dqkv_t)
    wide_rows(mixed, HD, mixed_t[...])
    add_projection(x, mixed, proj, adaln, result)
    backward_rest(x, cot, weight, adaln, normed, branch, mixed, dqkv_t, d_x, slabs, *rest)


def spatial_backward(x, cot, weight, proj, adaln, gains, qkv_t, mixed, d_x, slabs,
                     normed, branch, dmixed_t, dqkv_t, *rest):
    norm_tokens(x, adaln, normed)
    gate_cotangent(cot, adaln, branch)
    dmixed_t[...] = jnp.dot(branch[...], proj[...], preferred_element_type=F32).T
    heads_loop(qkv_t, gains, None, dmixed_t, dqkv_t)
    backward_rest(x, cot, weight, adaln, normed, branch, mixed, dqkv_t, d_x, slabs, *rest)


TOKEN_SHAPE = ((TOKENS, MODEL), BF16)
SLAB_SHAPE = ((SHARDS, SLAB, 128), BF16)
QKV_T = ((3 * HD, TOKENS), F32)
HEADS_T = ((HD, TOKENS), F32)
MIXED = ((TOKENS, PROJ_TILES * 128), BF16)
REST = [((TOKENS, QKV_TILES * 128), BF16), ((TOKENS, MODEL), F32), ((MODEL, TOKENS), BF16),
        ((TILES * MODEL, 128), F32)]


def stage(kernel, outs, scratch, *operands):
    return pl.pallas_call(
        kernel,
        out_shape=[jax.ShapeDtypeStruct(*o) for o in outs],
        in_specs=[pl.BlockSpec(memory_space=pltpu.VMEM)] * len(operands),
        out_specs=[pl.BlockSpec(memory_space=pltpu.VMEM)] * len(outs),
        scratch_shapes=[pltpu.VMEM(*s) for s in scratch],
        compiler_params=pltpu.CompilerParams(vmem_limit_bytes=62 << 20),
        name=kernel.__name__,
    )(*operands)


def run_spatial_forward(*operands):
    return stage(spatial_forward, [TOKEN_SHAPE, QKV_T, MIXED], [TOKEN_SHAPE, HEADS_T], *operands)


def run_temporal(*operands):
    return stage(temporal_both, [TOKEN_SHAPE, TOKEN_SHAPE, SLAB_SHAPE],
                 [TOKEN_SHAPE, QKV_T, HEADS_T, MIXED, TOKEN_SHAPE, HEADS_T, QKV_T] + REST, *operands)


def run_spatial_backward(*operands):
    return stage(spatial_backward, [TOKEN_SHAPE, SLAB_SHAPE],
                 [TOKEN_SHAPE, TOKEN_SHAPE, HEADS_T, QKV_T] + REST, *operands)


MESH = pl.DeviceIdType.MESH
ORDERS = (("y", "z", "x"), ("z", "x", "y"), ("x", "y", "z"))
ROWS = ((0, 64), (64, 64), (128, 48))
PARTS = tuple((which, start, rows, ORDERS[i]) for which in range(2) for i, (start, rows) in enumerate(ROWS))
COUNT = len(PARTS)


def place():
    wide = lax.axis_index("wide")
    narrow = lax.axis_index("narrow")
    x_lo, y, core = wide // 8, (wide // 2) % 4, wide % 2
    z, x_hi = narrow // 2, narrow % 2
    return {"x": x_hi * 2 + x_lo, "y": y, "z": z, "core": core}


def device_of(at):
    wide = (at["x"] % 2) * 8 + at["y"] * 2 + at["core"]
    narrow = at["z"] * 2 + at["x"] // 2
    return (wide, narrow)


def moved(at, axis, step):
    size = 2 if axis == "core" else 4
    return {**at, axis: (at[axis] + step) % size}


def add_rows(count, target, sources, cast):
    def step(index, carry):
        total = sources[0](index).astype(jnp.float32)
        for source in sources[1:]:
            total = total + source(index).astype(jnp.float32)
        target(index, total.astype(cast))
        return carry

    lax.fori_loop(0, count, step, 0)


def scatter_kernel(scale, spatial, temporal, qkv_s, proj_s, qkv_t, proj_t, sums, *scratch):
    buffers = [scratch[i * COUNT:(i + 1) * COUNT] for i in range(8)]
    own, from_core, first, second, third, recv1, recv2, recv3 = buffers
    own_sem, core_send, core_recv, send_sem, recv_sem = scratch[8 * COUNT:]
    slabs = (spatial, temporal)
    at = place()
    partner = device_of(moved(at, "core", 1))
    core = at["core"]
    barrier = pltpu.get_barrier_semaphore()
    peers = [partner] + [device_of(moved(at, a, d)) for a in ("x", "y", "z") for d in (1, 3)]
    for peer in peers:
        pl.semaphore_signal(barrier, inc=1, device_id=peer, device_id_type=MESH)
    pl.semaphore_wait(barrier, len(peers))

    core_copies, own_copies = [], []
    for part in range(COUNT):
        which, start, count, _ = PARTS[part]
        rows = pl.ds(start, count)
        copy = pltpu.make_async_remote_copy(
            src_ref=slabs[which].at[:, :, 1 - core, :, :, rows],
            dst_ref=from_core[part],
            send_sem=core_send.at[part], recv_sem=core_recv.at[part],
            device_id=partner, device_id_type=MESH)
        copy.start()
        core_copies.append(copy)
        mine = pltpu.make_async_copy(slabs[which].at[:, :, core, :, :, rows], own[part], own_sem.at[part])
        mine.start()
        own_copies.append(mine)

    bufs = (first, second, third)
    recvs = (recv1, recv2, recv3)

    def halves(level, block):
        if level == 0:
            return block.at[0:2], block.at[2:4]
        if level == 1:
            return block.at[0:2], block.at[2:4]
        return block.at[0:32], block.at[32:block.shape[0]]

    pending = {}

    def copy_of(part, level, direction, kind, src, dst):
        step = 1 if direction == 0 else 3
        axis = PARTS[part][3][level]
        slot = ((part * 3 + level) * 2 + direction) * 3 + kind
        copy = pltpu.make_async_remote_copy(
            src_ref=src, dst_ref=dst,
            send_sem=send_sem.at[slot], recv_sem=recv_sem.at[slot],
            device_id=device_of(moved(at, axis, step)), device_id_type=MESH)
        copy.start()
        pending[(part, level, direction, kind)] = copy

    def start_level(part, level):
        axis = PARTS[part][3][level]
        here = at[axis]
        source = bufs[level][part]
        recv = recvs[level][part]
        for direction in (0, 1):
            relay_half, plain_half = direction, 1 - direction
            far = source.at[(here + 2) % 4]
            near = source.at[(here + (1 if direction == 0 else 3)) % 4]
            copy_of(part, level, direction, 0, halves(level, far)[relay_half],
                    halves(level, recv.at[direction, 0])[relay_half])
            copy_of(part, level, direction, 1, halves(level, near)[plain_half],
                    halves(level, recv.at[direction, 1])[plain_half])

    def relay_level(part, level):
        axis = PARTS[part][3][level]
        here = at[axis]
        source = bufs[level][part]
        recv = recvs[level][part]
        for direction in (0, 1):
            pending[(part, level, direction, 0)].wait_recv()
            near = halves(level, source.at[(here + (1 if direction == 0 else 3)) % 4])[direction]
            came = halves(level, recv.at[direction, 0])[direction]
            if level == 0:
                def target(i, v):
                    came[i // 4, i % 4] = v
                add_rows(8, target, [lambda i: came[i // 4, i % 4], lambda i: near[i // 4, i % 4]], jnp.bfloat16)
            elif level == 1:
                def target(i, v):
                    came[i] = v
                add_rows(2, target, [lambda i: came[i], lambda i: near[i]], jnp.bfloat16)
            else:
                came[...] = (came[...].astype(jnp.float32) + near[...].astype(jnp.float32)).astype(jnp.bfloat16)
            copy_of(part, level, direction, 2, came, halves(level, recv.at[direction, 1])[direction])

    def finish_level(part, level):
        axis = PARTS[part][3][level]
        here = at[axis]
        source = bufs[level][part].at[here]
        recv = recvs[level][part]
        for direction in (0, 1):
            pending[(part, level, direction, 1)].wait_recv()
            pending[(part, level, direction, 2)].wait_recv()
        plus, minus = recv.at[0, 1], recv.at[1, 1]
        if level == 0:
            goal = second[part]

            def target(i, v):
                goal[i // 4, i % 4] = v
            add_rows(16, target, [lambda i: source[i // 4, i % 4], lambda i: plus[i // 4, i % 4],
                                  lambda i: minus[i // 4, i % 4]], jnp.bfloat16)
        elif level == 1:
            goal = third[part]

            def target(i, v):
                goal[i] = v
            add_rows(4, target, [lambda i: source[i], lambda i: plus[i], lambda i: minus[i]], jnp.bfloat16)
        else:
            which, start, count, _ = PARTS[part]
            sums[which, start:start + count, :] = (
                source[...].astype(jnp.float32) + plus[...].astype(jnp.float32)
                + minus[...].astype(jnp.float32)) * scale

    for part in range(COUNT):
        core_copies[part].wait_recv()
        own_copies[part].wait()
        order = PARTS[part][3]

        def target(index, value):
            digit = {"x": (index % 2) * 2 + index // 32, "y": (index // 8) % 4, "z": (index // 2) % 4}
            first[part][digit[order[0]], digit[order[1]], digit[order[2]]] = value

        mine, theirs = own[part], from_core[part]
        add_rows(64, target,
                 [lambda i: mine[i // 32, (i // 8) % 4, (i // 2) % 4, i % 2],
                  lambda i: theirs[i // 32, (i // 8) % 4, (i // 2) % 4, i % 2]], jnp.bfloat16)
        start_level(part, 0)
    for level in range(3):
        for part in range(COUNT):
            relay_level(part, level)
        for part in range(COUNT):
            finish_level(part, level)
            if level < 2:
                start_level(part, level + 1)
    for copy in core_copies:
        copy.wait_send()
    for copy in pending.values():
        copy.wait_send()
    for which, (qkv, proj) in enumerate(((qkv_s, proj_s), (qkv_t, proj_t))):
        for tile in range(TILES):
            out, column = (qkv, tile * 128) if tile < QKV_TILES else (proj, (tile - QKV_TILES) * 128)
            width = min(128, out.shape[1] - column)
            ninth = 152 + tile if tile < 16 else 157 + tile
            out[0:8, column:column + width] = sums[which, tile * 8:tile * 8 + 8, :width]
            out[8:9, column:column + width] = sums[which, ninth:ninth + 1, :width]


def scatter_sums(spatial, temporal, scale):
    shaped = [a.reshape(2, 4, 2, 4, 2, SLAB, 128) for a in (spatial, temporal)]
    scratch = []
    for lead in ((2, 4, 4, 2), (2, 4, 4, 2), (4, 4, 4), (4, 4), (4,), (2, 2, 4, 4), (2, 2, 4), (2, 2)):
        scratch += [pltpu.VMEM(lead + (rows, 128), BF16) for _, _, rows, _ in PARTS]
    outs = [jax.ShapeDtypeStruct((9, 3 * HD), F32), jax.ShapeDtypeStruct((9, HD), F32)] * 2
    return pl.pallas_call(
        functools.partial(scatter_kernel, scale),
        out_shape=outs,
        in_specs=[pl.BlockSpec(memory_space=pl.ANY)] * 2,
        out_specs=[pl.BlockSpec(memory_space=pltpu.VMEM)] * 4,
        scratch_shapes=[pltpu.VMEM((2, SLAB, 128), F32)] + scratch + [
            pltpu.SemaphoreType.DMA((COUNT,)),
            pltpu.SemaphoreType.DMA((COUNT,)),
            pltpu.SemaphoreType.DMA((COUNT,)),
            pltpu.SemaphoreType.DMA((COUNT * 18,)),
            pltpu.SemaphoreType.DMA((COUNT * 18,)),
        ],
        compiler_params=pltpu.CompilerParams(collective_id=0, has_side_effects=True, vmem_limit_bytes=62 << 20),
        name="scatter_sums",
    )(*shaped)


def turn(tokens):
    moved_tokens = lax.all_to_all(tokens.reshape(2, SEQ, MODEL), ("wide", "narrow"), split_axis=1, concat_axis=0, tiled=True)
    return jnp.transpose(moved_tokens, (1, 0, 2)).reshape(TOKENS, MODEL)


def body(clip_tokens, cotangent, qkv_spatial, proj_spatial, adaln_spatial, qknorm_spatial,
         qkv_temporal, proj_temporal, adaln_temporal, qknorm_temporal):
    clip = clip_tokens.reshape(TOKENS, MODEL)
    cot = jnp.transpose(cotangent, (1, 0, 2)).reshape(TOKENS, MODEL)
    spatial = (qkv_spatial, proj_spatial, adaln_spatial, qknorm_spatial.T)
    temporal = (qkv_temporal, proj_temporal, adaln_temporal, qknorm_temporal.T)
    middle, qkv_t, mixed = run_spatial_forward(clip, *spatial)
    result, d_middle, slabs_t = run_temporal(turn(middle), cot, *temporal)
    grad_clip, slabs_s = run_spatial_backward(clip, turn(d_middle), *spatial, qkv_t, mixed)
    sums = scatter_sums(slabs_s, slabs_t, 1.0 / math.sqrt(SEQ * SEQ))
    result = jnp.transpose(result.reshape(2, SEQ, MODEL), (1, 0, 2))
    return (result, grad_clip.reshape(2, SEQ, MODEL), *sums)


def solution(mesh):
    in_specs = (
        P(("wide", "narrow"), None, None),
        P(None, ("wide", "narrow"), None),
        P(),
        P(),
        P(),
        P(),
        P(),
        P(),
        P(),
        P(),
    )
    out_specs = (
        P(None, ("wide", "narrow"), None),
        P(("wide", "narrow"), None, None),
        P(("wide", "narrow"), None),
        P(("wide", "narrow"), None),
        P(("wide", "narrow"), None),
        P(("wide", "narrow"), None),
    )
    return jax.shard_map(body, mesh=mesh, in_specs=in_specs, out_specs=out_specs, check_vma=False)
```

```python
import functools
import math

import jax
import jax.numpy as jnp
from jax import lax
from jax.experimental import pallas as pl
from jax.experimental.pallas import tpu as pltpu
from jax.sharding import PartitionSpec as P

HDIM = 72
HEADS = 8
HD = HDIM * HEADS
MODEL = 1152
LANE_TILES = MODEL // 128
TOKENS = 512
SEQ = 256
EPSILON = 1e-06
QKV_TILES, PROJ_TILES = 14, 5
SHARDS = 128
MESSAGE = 40
NT = (((1,), (1,)), ((), ()))
TN = (((0,), (0,)), ((), ()))
F32, BF16 = jnp.float32, jnp.bfloat16
MESH = pl.DeviceIdType.MESH
PARTS = ((0, 7, 64, ("y", "z", "x")), (7, 7, 64, ("z", "x", "y")), (14, 5, 48, ("x", "y", "z")))
COUNT = len(PARTS)


def place():
    wide = lax.axis_index("wide")
    narrow = lax.axis_index("narrow")
    x_lo, y, core = wide // 8, (wide // 2) % 4, wide % 2
    z, x_hi = narrow // 2, narrow % 2
    return {"x": x_hi * 2 + x_lo, "y": y, "z": z, "core": core}


def device_of(at):
    wide = (at["x"] % 2) * 8 + at["y"] * 2 + at["core"]
    narrow = at["z"] * 2 + at["x"] // 2
    return (wide, narrow)


def moved(at, axis, step):
    size = 2 if axis == "core" else 4
    return {**at, axis: (at[axis] + step) % size}


def row_loop(total, step, body, unroll=1):
    lax.fori_loop(0, total // step, lambda i, c: (body(pl.ds(pl.multiple_of(i * step, step), step)), c)[1], 0,
                  unroll=unroll)


def flat_rows(ref):
    return lambda rows: ref[rows, :].astype(F32)


def tile_rows(ref):
    return lambda rows: jnp.concatenate(
        [ref[pl.ds(pl.multiple_of(t * TOKENS + rows.start, 8), rows.size), :] for t in range(LANE_TILES)], axis=1)


def put_tiles(ref, rows, value):
    for t in range(LANE_TILES):
        ref[pl.ds(pl.multiple_of(t * TOKENS + rows.start, 8), rows.size), :] = value[:, t * 128:t * 128 + 128]


def centred(x):
    centre = x - jnp.mean(x, axis=-1, keepdims=True)
    spread = jnp.mean(centre * centre, axis=-1, keepdims=True)
    scale = lax.rsqrt(spread + EPSILON)
    return centre * scale, scale


def norm_tokens(x, adaln, normed):
    def body(rows):
        hat, _ = centred(x(rows))
        normed[rows, :] = (hat * (1.0 + adaln[1:2, :]) + adaln[0:1, :]).astype(BF16)

    row_loop(TOKENS, 16, body, 4)


def project_qkv(weight_t, normed, qkv_t):
    def body(i, carry):
        rows = pl.ds(pl.multiple_of(i * 576, 64), 576)
        qkv_t[rows, :] = lax.dot_general(weight_t[rows, :], normed[...], NT, preferred_element_type=F32)
        return carry

    lax.fori_loop(0, 3, body, 0)


def gate_cotangent(cot, adaln, branch):
    def body(rows):
        branch[rows, :] = (adaln[2:3, :] * cot(rows)).astype(BF16)

    row_loop(TOKENS, 64, body)


def pull_mixed(proj_t, branch, dmixed_t):
    dmixed_t[...] = lax.dot_general(proj_t[...], branch[...], NT, preferred_element_type=F32)


def column(row):
    grid = (HDIM, HDIM)
    same = lax.broadcasted_iota(jnp.int32, grid, 0) == lax.broadcasted_iota(jnp.int32, grid, 1)
    return jnp.sum(jnp.where(same, jnp.broadcast_to(row, grid), 0.0), axis=1, keepdims=True)


def split3(value):
    high = value.astype(BF16).astype(F32)
    return high, value - high


def heads_loop(qkv_t, gains, mixed_t, dmixed_t):
    root = 1.0 / math.sqrt(HDIM)
    q_gain, k_gain = column(gains[0:1, :]), column(gains[1:2, :])

    def body(index, carry):
        head, seq = index // 2, index % 2
        lanes = pl.ds(pl.multiple_of(seq * SEQ, SEQ), SEQ)
        at = [pl.ds(pl.multiple_of(part * HD + head * HDIM, 8), HDIM) for part in range(3)]
        q, k, v = (qkv_t[rows, lanes] for rows in at)
        q_scale = lax.rsqrt(jnp.mean(q * q, axis=0, keepdims=True) + EPSILON)
        k_scale = lax.rsqrt(jnp.mean(k * k, axis=0, keepdims=True) + EPSILON)
        q_hat, k_hat = q * q_scale, k * k_scale
        qs, kn = q_hat * (q_gain * root), k_hat * k_gain
        q_high, q_low = split3(qs)
        k_high, k_low = split3(kn)
        q3 = jnp.concatenate([q_high, q_low, q_high], axis=0).astype(BF16)
        k3 = jnp.concatenate([k_high, k_high, k_low], axis=0).astype(BF16)
        raised = jnp.exp(lax.dot_general(k3, q3, TN, preferred_element_type=F32))
        inverse = 1.0 / jnp.sum(raised, axis=0, keepdims=True)
        v_low = v.astype(BF16)
        if mixed_t is not None:
            out = jnp.dot(v_low, raised.astype(BF16), preferred_element_type=F32) * inverse
            mixed_t[at[0], lanes] = out
        if dmixed_t is not None:
            weights = raised * inverse
            d_out = dmixed_t[at[0], lanes].astype(BF16)
            d_weights = lax.dot_general(v_low, d_out, TN, preferred_element_type=F32)
            shift = jnp.sum(weights * d_weights, axis=0, keepdims=True)
            d_scores = (weights * (d_weights - shift)).astype(BF16)
            dv = lax.dot_general(d_out, weights.astype(BF16), NT, preferred_element_type=F32)
            dq = jnp.dot(k_high.astype(BF16), d_scores, preferred_element_type=F32)
            dk = lax.dot_general(q_high.astype(BF16), d_scores, NT, preferred_element_type=F32)
            dq = dq * (q_gain * root)
            dk = dk * k_gain
            qkv_t[at[0], lanes] = q_scale * (dq - q_hat * jnp.mean(q_hat * dq, axis=0, keepdims=True))
            qkv_t[at[1], lanes] = k_scale * (dk - k_hat * jnp.mean(k_hat * dk, axis=0, keepdims=True))
            qkv_t[at[2], lanes] = dv
        return carry

    lax.fori_loop(0, 2 * HEADS, body, 0, unroll=2)


def wide_rows(source, used, ref):
    ref[:, :used] = source[...].T.astype(BF16)
    ref[:, used:] = jnp.zeros((TOKENS, ref.shape[1] - used), BF16)


def add_projection(x, mixed, proj_t, adaln, put):
    def body(rows):
        projected = jnp.dot(mixed[rows, :HD], proj_t[...], preferred_element_type=F32)
        put(rows, x(rows) + adaln[2:3, :] * projected)

    row_loop(TOKENS, 256, body)


def pull_norm(x, cot, dqkv, weight_t, adaln, work, put):
    third = MODEL // 3
    for i in range(3):
        work[i * TOKENS:(i + 1) * TOKENS, :third] = jnp.dot(
            dqkv[:, :3 * HD], weight_t[:, i * third:(i + 1) * third], preferred_element_type=F32)

    def body(rows):
        d_normed = jnp.concatenate(
            [work[pl.ds(pl.multiple_of(i * TOKENS + rows.start, 8), rows.size), :third] for i in range(3)], axis=1)
        hat, scale = centred(x(rows))
        u = d_normed * (1.0 + adaln[1:2, :])
        d_x = scale * (u - jnp.mean(u, axis=-1, keepdims=True) - hat * jnp.mean(u * hat, axis=-1, keepdims=True))
        put(rows, cot(rows) + d_x)

    row_loop(TOKENS, 16, body, 4)


def gradient_part(left, right, first_tile, tiles, slab, work):
    done = 0
    while done < tiles:
        size = min(2, tiles - done)
        lane = pl.multiple_of((first_tile + done) * 128, 128)
        out = jnp.dot(left[...], right[:, pl.ds(lane, size * 128)], preferred_element_type=F32)
        for t in range(size):
            work[(done + t) * MODEL:(done + t + 1) * MODEL, :] = out[:, t * 128:(t + 1) * 128]
        done += size
    skip = max(0, 8 - tiles)

    def gather(s, carry):
        rows = [work[pl.ds(t * MODEL + 9 * s, 8), :] for t in range(tiles)]
        rows.append(work[pl.ds(9 * s + 8, 8, stride=MODEL), :])
        slab[s // 64, (s // 16) % 4, (s // 8) % 2, (s // 2) % 4, s % 2] = jnp.concatenate(rows, axis=0).astype(BF16)
        return carry

    lax.fori_loop(0, SHARDS, gather, 0, unroll=2)


def pack_messages(source, send):
    top = lax.broadcasted_iota(jnp.int32, (8, 128), 0) < 2

    def body(s, carry):
        rows = [source[pl.ds(a * SEQ + 2 * s + b, 8, stride=TOKENS), :] for a in range(2) for b in range(2)]
        last = 8 * TOKENS + 2 * s
        rows.append(jnp.where(top, source[pl.ds(last, 8), :], source[pl.ds(last + SEQ - 2, 8), :]))
        send[s] = jnp.concatenate(rows, axis=0).astype(BF16)
        return carry

    lax.fori_loop(0, SHARDS, body, 0, unroll=4)


def unpack_messages(recv, target):
    def body(s, carry):
        rows = recv[s].astype(F32)
        for a in range(2):
            for b in range(2):
                at = (a * 2 + b) * 8
                target[pl.ds(b * SEQ + 2 * s + a, 8, stride=TOKENS), :] = rows[at:at + 8]
            target[pl.ds(8 * TOKENS + 2 * s + a, 2, stride=SEQ), :] = rows[32 + 2 * a:34 + 2 * a]
        return carry

    lax.fori_loop(0, SHARDS, body, 0, unroll=4)


def start_exchange(me, send, recv, send_sem, recv_sem, own_sem):
    def body(step, carry):
        other = (me + step) % SHARDS
        pltpu.make_async_remote_copy(
            src_ref=send.at[other], dst_ref=recv.at[me], send_sem=send_sem, recv_sem=recv_sem,
            device_id=(other // 8, other % 8), device_id_type=MESH).start()
        return carry

    lax.fori_loop(1, SHARDS, body, 0)
    own = pltpu.make_async_copy(send.at[me], recv.at[me], own_sem)
    own.start()
    every = pltpu.make_async_remote_copy(
        src_ref=send.at[pl.ds(0, SHARDS - 1)], dst_ref=recv.at[pl.ds(0, SHARDS - 1)],
        send_sem=send_sem, recv_sem=recv_sem, device_id=((me + 1) % SHARDS // 8, (me + 1) % SHARDS % 8),
        device_id_type=MESH)
    return own, every


def add_rows(count, target, sources):
    def step(index, carry):
        total = sources[0](index).astype(F32)
        for source in sources[1:]:
            total = total + source(index).astype(F32)
        target(index, total.astype(BF16))
        return carry

    lax.fori_loop(0, count, step, 0)


class Scatter:
    def __init__(self, at, slabs, buffers, sems, base, sums, which, scale):
        self.at, self.slabs, self.sums, self.which, self.scale = at, slabs, sums, which, scale
        self.from_core, self.first, self.second, self.third, *recvs = [
            buffers[i * COUNT:(i + 1) * COUNT] for i in range(7)]
        self.bufs, self.recvs = (self.first, self.second, self.third), recvs
        self.send_sem, self.recv_sem = sems
        self.base = base
        self.core, self.flying = {}, {}

    def copy(self, key, slot, src, dst, axis, step):
        slot = self.base + slot
        made = pltpu.make_async_remote_copy(
            src_ref=src, dst_ref=dst, send_sem=self.send_sem.at[slot], recv_sem=self.recv_sem.at[slot],
            device_id=device_of(moved(self.at, axis, step)), device_id_type=MESH)
        made.start()
        self.flying[key] = made

    def begin(self, part):
        self.copy((part, "core"), COUNT * 18 + part, self.slabs[part].at[:, :, 1 - self.at["core"]],
                  self.from_core[part], "core", 1)

    def join_cores(self, part):
        self.flying[(part, "core")].wait_recv()
        order, first = PARTS[part][3], self.first[part]
        mine, theirs, core = self.slabs[part], self.from_core[part], self.at["core"]

        def target(i, value):
            digit = {"x": (i % 2) * 2 + i // 32, "y": (i // 8) % 4, "z": (i // 2) % 4}
            first[digit[order[0]], digit[order[1]], digit[order[2]]] = value

        add_rows(64, target, [lambda i: mine[i // 32, (i // 8) % 4, core, (i // 2) % 4, i % 2],
                              lambda i: theirs[i // 32, (i // 8) % 4, (i // 2) % 4, i % 2]])
        self.start(part, 0)

    @staticmethod
    def halves(level, block):
        cut = 2 if level < 2 else 32
        return block.at[0:cut], block.at[cut:block.shape[0]]

    def start(self, part, level):
        axis = PARTS[part][3][level]
        here, source, recv = self.at[axis], self.bufs[level][part], self.recvs[level][part]
        for direction in (0, 1):
            step = 3 if direction else 1
            relay, plain = direction, 1 - direction
            far, near = source.at[(here + 2) % 4], source.at[(here + step) % 4]
            slot = ((part * 3 + level) * 2 + direction) * 3
            self.copy((part, level, direction, 0), slot, self.halves(level, far)[relay],
                      self.halves(level, recv.at[direction, 0])[relay], axis, step)
            self.copy((part, level, direction, 1), slot + 1, self.halves(level, near)[plain],
                      self.halves(level, recv.at[direction, 1])[plain], axis, step)

    def relay(self, part, level):
        axis = PARTS[part][3][level]
        here, source, recv = self.at[axis], self.bufs[level][part], self.recvs[level][part]
        for direction in (0, 1):
            step = 3 if direction else 1
            self.flying[(part, level, direction, 0)].wait_recv()
            near = self.halves(level, source.at[(here + step) % 4])[direction]
            came = self.halves(level, recv.at[direction, 0])[direction]
            if level == 0:
                def target(i, v):
                    came[i // 4, i % 4] = v
                add_rows(8, target, [lambda i: came[i // 4, i % 4], lambda i: near[i // 4, i % 4]])
            elif level == 1:
                def target(i, v):
                    came[i] = v
                add_rows(2, target, [lambda i: came[i], lambda i: near[i]])
            else:
                came[...] = (came[...].astype(F32) + near[...].astype(F32)).astype(BF16)
            slot = ((part * 3 + level) * 2 + direction) * 3 + 2
            self.copy((part, level, direction, 2), slot, came, self.halves(level, recv.at[direction, 1])[direction],
                      axis, step)

    def finish(self, part, level):
        axis = PARTS[part][3][level]
        source, recv = self.bufs[level][part].at[self.at[axis]], self.recvs[level][part]
        for direction in (0, 1):
            self.flying[(part, level, direction, 1)].wait_recv()
            self.flying[(part, level, direction, 2)].wait_recv()
        plus, minus = recv.at[0, 1], recv.at[1, 1]
        if level == 0:
            goal = self.second[part]

            def target(i, v):
                goal[i // 4, i % 4] = v
            add_rows(16, target, [lambda i: source[i // 4, i % 4], lambda i: plus[i // 4, i % 4],
                                  lambda i: minus[i // 4, i % 4]])
        elif level == 1:
            goal = self.third[part]

            def target(i, v):
                goal[i] = v
            add_rows(4, target, [lambda i: source[i], lambda i: plus[i], lambda i: minus[i]])
        else:
            start = sum(p[2] for p in PARTS[:part])
            self.sums[self.which, start:start + PARTS[part][2], :] = (
                source[...].astype(F32) + plus[...].astype(F32) + minus[...].astype(F32)) * self.scale
        if level < 2:
            self.start(part, level + 1)

    def drain(self):
        for made in self.flying.values():
            made.wait_send()


def parts_step(step, *level):
    for part in range(COUNT):
        step(part, *level)


def both_blocks(scale, clip_hbm, cot_hbm, wt_s_hbm, pt_s_hbm, adaln_s, gains_s, wt_t_hbm, pt_t_hbm, adaln_t, gains_t,
                result, grad_clip, sums,
                clip, cot, wt_s, pt_s, wt_t, pt_t, normed_s, normed_t, branch, qkv_s, qkv_t, mixed_f, dmixed_f,
                mixed_s, mixed_t, dqkv, left, work, tokens_a, tokens_b, send, recv_a, recv_b, slab0, slab1, slab2,
                *rest):
    buffers = rest[:7 * COUNT]
    load_sem, own_sem, send_a, send_b, got_a, got_b, sum_send, sum_recv, free_sem = rest[7 * COUNT:]
    at = place()
    me = lax.axis_index("wide") * 8 + lax.axis_index("narrow")
    loads = []
    for i, (hbm, vmem) in enumerate(((clip_hbm, clip), (wt_s_hbm, wt_s), (pt_s_hbm, pt_s), (cot_hbm, cot),
                                     (pt_t_hbm, pt_t), (wt_t_hbm, wt_t))):
        load = pltpu.make_async_copy(hbm, vmem, load_sem.at[i])
        load.start()
        loads.append(load)
    barrier = pltpu.get_barrier_semaphore()

    def greet(step, carry):
        other = (me + step) % SHARDS
        pl.semaphore_signal(barrier, inc=1, device_id=(other // 8, other % 8), device_id_type=MESH)
        return carry

    lax.fori_loop(1, SHARDS, greet, 0)

    loads[0].wait()
    norm_tokens(flat_rows(clip), adaln_s, normed_s)
    loads[1].wait()
    project_qkv(wt_s, normed_s, qkv_s)
    heads_loop(qkv_s, gains_s, mixed_f, None)
    wide_rows(mixed_f, HD, mixed_s)
    loads[2].wait()
    add_projection(flat_rows(clip), mixed_s, pt_s, adaln_s, functools.partial(put_tiles, tokens_a))
    pack_messages(tokens_a, send)
    pl.semaphore_wait(barrier, SHARDS - 1)
    own, every = start_exchange(me, send, recv_a, send_a, got_a, own_sem.at[0])

    loads[3].wait()
    gate_cotangent(flat_rows(cot), adaln_t, branch)
    loads[4].wait()
    pull_mixed(pt_t, branch, dmixed_f)
    loads[5].wait()
    own.wait()
    every.wait_recv()
    unpack_messages(recv_a, tokens_b)
    middle = tile_rows(tokens_b)
    norm_tokens(middle, adaln_t, normed_t)
    project_qkv(wt_t, normed_t, qkv_t)
    heads_loop(qkv_t, gains_t, mixed_f, dmixed_f)
    wide_rows(qkv_t, 3 * HD, dqkv)
    pull_norm(middle, flat_rows(cot), dqkv, wt_t, adaln_t, qkv_t, functools.partial(put_tiles, tokens_a))
    every.wait_send()
    pack_messages(tokens_a, send)
    own, every = start_exchange(me, send, recv_b, send_b, got_b, own_sem.at[1])
    wide_rows(mixed_f, HD, mixed_t)

    def put_result(rows, value):
        result[rows, :] = value.astype(BF16)

    slabs = (slab0, slab1, slab2)
    sems = (sum_send, sum_recv)
    sum_t = Scatter(at, slabs, buffers, sems, 0, sums, 1, scale)
    left[...] = normed_t[...].T
    for part in (0, 1):
        gradient_part(left, dqkv, PARTS[part][0], PARTS[part][1], slabs[part], work)
        sum_t.begin(part)
    left[...] = branch[...].T
    gradient_part(left, mixed_t, 0, PROJ_TILES, slabs[2], work)
    sum_t.begin(2)
    add_projection(middle, mixed_t, pt_t, adaln_t, put_result)

    own.wait()
    every.wait_recv()
    unpack_messages(recv_b, tokens_b)
    d_middle = tile_rows(tokens_b)
    gate_cotangent(d_middle, adaln_s, branch)
    pull_mixed(pt_s, branch, dmixed_f)
    parts_step(sum_t.join_cores)
    heads_loop(qkv_s, gains_s, None, dmixed_f)
    parts_step(sum_t.relay, 0)
    wide_rows(qkv_s, 3 * HD, dqkv)
    parts_step(sum_t.finish, 0)

    def put_grad(rows, value):
        grad_clip[rows, :] = value.astype(BF16)

    left[...] = normed_s[...].T
    parts_step(sum_t.relay, 1)
    pull_norm(flat_rows(clip), d_middle, dqkv, wt_s, adaln_s, qkv_s, put_grad)
    parts_step(sum_t.finish, 1)
    parts_step(sum_t.relay, 2)
    parts_step(sum_t.finish, 2)
    sum_t.drain()
    peers = [device_of(moved(at, "core", 1))] + [device_of(moved(at, a, d)) for a in ("x", "y", "z") for d in (1, 3)]
    for peer in peers:
        pl.semaphore_signal(free_sem, inc=1, device_id=peer, device_id_type=MESH)
    sum_s = Scatter(at, slabs, buffers, sems, COUNT * 19, sums, 0, scale)
    gradient_part(left, dqkv, PARTS[0][0], PARTS[0][1], slabs[0], work)
    pl.semaphore_wait(free_sem, len(peers))
    sum_s.begin(0)
    gradient_part(left, dqkv, PARTS[1][0], PARTS[1][1], slabs[1], work)
    sum_s.begin(1)
    sum_s.join_cores(0)
    left[...] = branch[...].T
    gradient_part(left, mixed_s, 0, PROJ_TILES, slabs[2], work)
    sum_s.begin(2)
    sum_s.join_cores(1)
    sum_s.join_cores(2)
    for level in range(3):
        parts_step(sum_s.relay, level)
        parts_step(sum_s.finish, level)
    sum_s.drain()
    every.wait_send()


def split_sums(sums, qkv_s, proj_s, qkv_t, proj_t):
    for which, outs in enumerate(((qkv_s, proj_s), (qkv_t, proj_t))):
        start = 0
        for first, tiles, rows, _ in PARTS:
            out, base = (outs[0], 0) if first < QKV_TILES else (outs[1], QKV_TILES)
            for t in range(tiles):
                lane = (first + t - base) * 128
                width = min(128, out.shape[1] - lane)
                out[0:8, lane:lane + width] = sums[which, start + 8 * t:start + 8 * t + 8, :width]
                ninth = start + 8 * tiles + t
                out[8:9, lane:lane + width] = sums[which, ninth:ninth + 1, :width]
            start += rows


def run_blocks(scale, clip, cot, wt_s, pt_s, adaln_s, gains_s, wt_t, pt_t, adaln_t, gains_t):
    token, qkv_f, heads_f = ((TOKENS, MODEL), BF16), ((3 * HD, TOKENS), F32), ((HD, TOKENS), F32)
    tiles = ((LANE_TILES * TOKENS, 128), F32)
    mixed, message = ((TOKENS, PROJ_TILES * 128), BF16), ((SHARDS, MESSAGE, 128), BF16)
    shapes = [token, token, ((3 * HD, MODEL), BF16), ((HD, MODEL), BF16), ((3 * HD, MODEL), BF16), ((HD, MODEL), BF16),
              token, token, token, qkv_f, qkv_f, heads_f, heads_f, mixed, mixed, ((TOKENS, QKV_TILES * 128), BF16),
              ((MODEL, TOKENS), BF16), ((8 * MODEL, 128), F32), ((LANE_TILES * TOKENS + 8, 128), F32), tiles, message, message, message]
    shapes += [((2, 4, 2, 4, 2, rows, 128), BF16) for _, _, rows, _ in PARTS]
    for lead in ((2, 4, 4, 2), (4, 4, 4), (4, 4), (4,), (2, 2, 4, 4), (2, 2, 4), (2, 2)):
        shapes += [(lead + (rows, 128), BF16) for _, _, rows, _ in PARTS]
    vmem, hbm = pl.BlockSpec(memory_space=pltpu.VMEM), pl.BlockSpec(memory_space=pl.ANY)
    return pl.pallas_call(
        functools.partial(both_blocks, scale),
        out_shape=[jax.ShapeDtypeStruct(*token), jax.ShapeDtypeStruct(*token), jax.ShapeDtypeStruct((2, 176, 128), F32)],
        in_specs=[hbm, hbm, hbm, hbm, vmem, vmem, hbm, hbm, vmem, vmem],
        out_specs=[vmem] * 3,
        scratch_shapes=[pltpu.VMEM(*s) for s in shapes] + [
            pltpu.SemaphoreType.DMA((6,)), pltpu.SemaphoreType.DMA((2,)),
            pltpu.SemaphoreType.DMA, pltpu.SemaphoreType.DMA, pltpu.SemaphoreType.DMA, pltpu.SemaphoreType.DMA,
            pltpu.SemaphoreType.DMA((2 * COUNT * 19,)), pltpu.SemaphoreType.DMA((2 * COUNT * 19,)),
            pltpu.SemaphoreType.REGULAR],
        compiler_params=pltpu.CompilerParams(collective_id=0, has_side_effects=True, vmem_limit_bytes=67043328),
        name="both_blocks",
    )(clip, cot, wt_s, pt_s, adaln_s, gains_s, wt_t, pt_t, adaln_t, gains_t)


def body(clip_tokens, cotangent, qkv_spatial, proj_spatial, adaln_spatial, qknorm_spatial,
         qkv_temporal, proj_temporal, adaln_temporal, qknorm_temporal):
    clip = clip_tokens.reshape(TOKENS, MODEL)
    cot = jnp.transpose(cotangent, (1, 0, 2)).reshape(TOKENS, MODEL)
    result, grad_clip, sums = run_blocks(
        1.0 / math.sqrt(SEQ * SEQ), clip, cot, qkv_spatial.T, proj_spatial.T, adaln_spatial, qknorm_spatial,
        qkv_temporal.T, proj_temporal.T, adaln_temporal, qknorm_temporal)
    grads = pl.pallas_call(
        split_sums,
        out_shape=[jax.ShapeDtypeStruct((9, 3 * HD), F32), jax.ShapeDtypeStruct((9, HD), F32)] * 2,
        in_specs=[pl.BlockSpec(memory_space=pltpu.VMEM)],
        out_specs=[pl.BlockSpec(memory_space=pltpu.VMEM)] * 4,
        name="split_sums",
    )(sums)
    result = jnp.transpose(result.reshape(2, SEQ, MODEL), (1, 0, 2))
    return (result, grad_clip.reshape(2, SEQ, MODEL), *grads)


def solution(mesh):
    in_specs = (
        P(("wide", "narrow"), None, None),
        P(None, ("wide", "narrow"), None),
        P(),
        P(),
        P(),
        P(),
        P(),
        P(),
        P(),
        P(),
    )
    out_specs = (
        P(None, ("wide", "narrow"), None),
        P(("wide", "narrow"), None, None),
        P(("wide", "narrow"), None),
        P(("wide", "narrow"), None),
        P(("wide", "narrow"), None),
        P(("wide", "narrow"), None),
    )
    return jax.shard_map(body, mesh=mesh, in_specs=in_specs, out_specs=out_specs, check_vma=False)
```

```python
import functools
import math

import jax
import jax.numpy as jnp
from jax import lax
from jax.experimental import pallas as pl
from jax.experimental.pallas import tpu as pltpu
from jax.sharding import PartitionSpec as P

HDIM = 72
HEADS = 8
HD = HDIM * HEADS
MODEL = 1152
LANE_TILES = MODEL // 128
TOKENS = 512
SEQ = 256
EPSILON = 1e-06
QKV_TILES, PROJ_TILES = 14, 5
SHARDS = 128
MESSAGE = 40
NT = (((1,), (1,)), ((), ()))
TN = (((0,), (0,)), ((), ()))
F32, BF16 = jnp.float32, jnp.bfloat16
MESH = pl.DeviceIdType.MESH
PARTS = ((0, 7, 64, ("y", "z", "x")), (7, 7, 64, ("z", "x", "y")), (14, 5, 48, ("x", "y", "z")))
COUNT = len(PARTS)


def place():
    wide = lax.axis_index("wide")
    narrow = lax.axis_index("narrow")
    x_lo, y, core = wide // 8, (wide // 2) % 4, wide % 2
    z, x_hi = narrow // 2, narrow % 2
    return {"x": x_hi * 2 + x_lo, "y": y, "z": z, "core": core}


def device_of(at):
    wide = (at["x"] % 2) * 8 + at["y"] * 2 + at["core"]
    narrow = at["z"] * 2 + at["x"] // 2
    return (wide, narrow)


def moved(at, axis, step):
    size = 2 if axis == "core" else 4
    return {**at, axis: (at[axis] + step) % size}


def row_loop(total, step, body, unroll=1):
    lax.fori_loop(0, total // step, lambda i, c: (body(pl.ds(pl.multiple_of(i * step, step), step)), c)[1], 0,
                  unroll=unroll)


def flat_rows(ref):
    return lambda rows: ref[rows, :].astype(F32)


def tile_rows(ref):
    return lambda rows: jnp.concatenate(
        [ref[pl.ds(pl.multiple_of(t * TOKENS + rows.start, 8), rows.size), :] for t in range(LANE_TILES)], axis=1)


def put_tiles(ref, rows, value):
    for t in range(LANE_TILES):
        ref[pl.ds(pl.multiple_of(t * TOKENS + rows.start, 8), rows.size), :] = value[:, t * 128:t * 128 + 128]


def centred(x):
    centre = x - jnp.mean(x, axis=-1, keepdims=True)
    spread = jnp.mean(centre * centre, axis=-1, keepdims=True)
    scale = lax.rsqrt(spread + EPSILON)
    return centre * scale, scale


def norm_tokens(x, adaln, normed):
    def body(rows):
        hat, _ = centred(x(rows))
        normed[rows, :] = (hat * (1.0 + adaln[1:2, :]) + adaln[0:1, :]).astype(BF16)

    row_loop(TOKENS, 16, body, 4)


def project_qkv(weight_t, normed, qkv_t):
    def body(i, carry):
        rows = pl.ds(pl.multiple_of(i * 576, 64), 576)
        qkv_t[rows, :] = lax.dot_general(weight_t[rows, :], normed[...], NT, preferred_element_type=F32)
        return carry

    lax.fori_loop(0, 3, body, 0)


def gate_cotangent(cot, adaln, branch):
    def body(rows):
        branch[rows, :] = (adaln[2:3, :] * cot(rows)).astype(BF16)

    row_loop(TOKENS, 64, body)


def pull_mixed(proj_t, branch, dmixed_t):
    dmixed_t[...] = lax.dot_general(proj_t[...], branch[...], NT, preferred_element_type=F32)


def column(row):
    grid = (HDIM, HDIM)
    same = lax.broadcasted_iota(jnp.int32, grid, 0) == lax.broadcasted_iota(jnp.int32, grid, 1)
    return jnp.sum(jnp.where(same, jnp.broadcast_to(row, grid), 0.0), axis=1, keepdims=True)


def split3(value):
    high = value.astype(BF16).astype(F32)
    return high, value - high


def heads_loop(qkv_t, gains, mixed_t, dmixed_t, first=0, last=2, unroll=1):
    root = 1.0 / math.sqrt(HDIM)
    q_gain, k_gain = column(gains[0:1, :]), column(gains[1:2, :])

    def one(head, seq):
        lanes = pl.ds(pl.multiple_of(seq * SEQ, SEQ), SEQ)
        at = [pl.ds(pl.multiple_of(part * HD + head * HDIM, 8), HDIM) for part in range(3)]
        loaded = [qkv_t[rows, lanes] for rows in at]
        loaded.append(None if dmixed_t is None else dmixed_t[at[0], lanes])
        return at, lanes, loaded

    def compute(at, lanes, loaded):
        q, k, v, d_mixed = loaded
        stores = []
        q_scale = lax.rsqrt(jnp.mean(q * q, axis=0, keepdims=True) + EPSILON)
        k_scale = lax.rsqrt(jnp.mean(k * k, axis=0, keepdims=True) + EPSILON)
        q_hat, k_hat = q * q_scale, k * k_scale
        qs, kn = q_hat * (q_gain * root), k_hat * k_gain
        q_high, q_low = split3(qs)
        k_high, k_low = split3(kn)
        q3 = jnp.concatenate([q_high, q_low, q_high], axis=0).astype(BF16)
        k3 = jnp.concatenate([k_high, k_high, k_low], axis=0).astype(BF16)
        raised = jnp.exp(lax.dot_general(k3, q3, TN, preferred_element_type=F32))
        inverse = 1.0 / jnp.sum(raised, axis=0, keepdims=True)
        v_low = v.astype(BF16)
        if mixed_t is not None:
            out = jnp.dot(v_low, raised.astype(BF16), preferred_element_type=F32) * inverse
            stores.append((mixed_t, at[0], out))
        if dmixed_t is not None:
            weights = raised * inverse
            d_out = d_mixed.astype(BF16)
            d_weights = lax.dot_general(v_low, d_out, TN, preferred_element_type=F32)
            shift = jnp.sum(weights * d_weights, axis=0, keepdims=True)
            d_scores = (weights * (d_weights - shift)).astype(BF16)
            dv = jnp.dot(weights.astype(BF16), d_out.T, preferred_element_type=F32).T
            dq = jnp.dot(k_high.astype(BF16), d_scores, preferred_element_type=F32)
            dk = jnp.dot(d_scores, q_high.astype(BF16).T, preferred_element_type=F32).T
            dq = dq * (q_gain * root)
            dk = dk * k_gain
            stores.append((qkv_t, at[0], q_scale * (dq - q_hat * jnp.mean(q_hat * dq, axis=0, keepdims=True))))
            stores.append((qkv_t, at[1], k_scale * (dk - k_hat * jnp.mean(k_hat * dk, axis=0, keepdims=True))))
            stores.append((qkv_t, at[2], dv))
        return lanes, stores

    def body(index, carry):
        taken = [one(index * 4 + i // 2, i % 2) for i in range(8)]
        for lanes, stores in [compute(*t) for t in taken]:
            for ref, rows, value in stores:
                ref[rows, lanes] = value
        return carry

    lax.fori_loop(first, last, body, 0, unroll=unroll)


def wide_rows(source, used, ref):
    ref[:, :used] = source[...].T.astype(BF16)
    ref[:, used:] = jnp.zeros((TOKENS, ref.shape[1] - used), BF16)


def add_projection(x, mixed, proj_t, adaln, put):
    def body(rows):
        projected = jnp.dot(mixed[rows, :HD], proj_t[...], preferred_element_type=F32)
        put(rows, x(rows) + adaln[2:3, :] * projected)

    row_loop(TOKENS, 256, body)


def pull_norm(x, cot, dqkv, weight_t, adaln, work, put):
    third = MODEL // 3
    for i in range(3):
        work[i * TOKENS:(i + 1) * TOKENS, :third] = jnp.dot(
            dqkv[:, :3 * HD], weight_t[:, i * third:(i + 1) * third], preferred_element_type=F32)

    def body(rows):
        d_normed = jnp.concatenate(
            [work[pl.ds(pl.multiple_of(i * TOKENS + rows.start, 8), rows.size), :third] for i in range(3)], axis=1)
        hat, scale = centred(x(rows))
        u = d_normed * (1.0 + adaln[1:2, :])
        d_x = scale * (u - jnp.mean(u, axis=-1, keepdims=True) - hat * jnp.mean(u * hat, axis=-1, keepdims=True))
        put(rows, cot(rows) + d_x)

    row_loop(TOKENS, 16, body, 4)


def gradient_part(left, right, first_tile, tiles, slab, work):
    done = 0
    while done < tiles:
        size = min(2, tiles - done)
        lane = pl.multiple_of((first_tile + done) * 128, 128)
        out = jnp.dot(left[...], right[:, pl.ds(lane, size * 128)], preferred_element_type=F32)
        for t in range(size):
            work[(done + t) * MODEL:(done + t + 1) * MODEL, :] = out[:, t * 128:(t + 1) * 128]
        done += size

    pad = slab.shape[-2] - 8 * tiles - 8

    def gather(wide, carry):
        goal, base = slab.at[wide // 8, (wide // 2) % 4, wide % 2], pl.multiple_of(wide * 72, 8)
        for narrow in range(8):
            at = base + 9 * narrow
            rows = [work[pl.ds(t * MODEL + at, 8), :] for t in range(tiles)]
            rows.append(work[pl.ds(at + 8, 8, stride=MODEL), :])
            if pad:
                rows.append(jnp.zeros((pad, 128), F32))
            goal[narrow // 2, narrow % 2] = jnp.concatenate(rows, axis=0).astype(BF16)
        return carry

    lax.fori_loop(0, SHARDS // 8, gather, 0)


def pack_messages(source, send):
    top = lax.broadcasted_iota(jnp.int32, (8, 128), 0) < 2

    def body(s, carry):
        rows = [source[pl.ds(a * SEQ + 2 * s + b, 8, stride=TOKENS), :] for a in range(2) for b in range(2)]
        last = 8 * TOKENS + 2 * s
        rows.append(jnp.where(top, source[pl.ds(last, 8), :], source[pl.ds(last + SEQ - 2, 8), :]))
        send[s] = jnp.concatenate(rows, axis=0).astype(BF16)
        return carry

    lax.fori_loop(0, SHARDS, body, 0, unroll=4)


def unpack_messages(recv, target):
    def body(s, carry):
        rows = recv[s].astype(F32)
        for a in range(2):
            for b in range(2):
                at = (a * 2 + b) * 8
                target[pl.ds(b * SEQ + 2 * s + a, 8, stride=TOKENS), :] = rows[at:at + 8]
            target[pl.ds(8 * TOKENS + 2 * s + a, 2, stride=SEQ), :] = rows[32 + 2 * a:34 + 2 * a]
        return carry

    lax.fori_loop(0, SHARDS, body, 0, unroll=4)


def start_exchange(me, send, recv, send_sem, recv_sem, own_sem):
    def body(step, carry):
        other = (me + step * 37) % SHARDS
        pltpu.make_async_remote_copy(
            src_ref=send.at[other], dst_ref=recv.at[me], send_sem=send_sem, recv_sem=recv_sem,
            device_id=(other // 8, other % 8), device_id_type=MESH).start()
        return carry

    lax.fori_loop(1, SHARDS, body, 0)
    own = pltpu.make_async_copy(send.at[me], recv.at[me], own_sem)
    own.start()
    every = pltpu.make_async_remote_copy(
        src_ref=send.at[pl.ds(0, SHARDS - 1)], dst_ref=recv.at[pl.ds(0, SHARDS - 1)],
        send_sem=send_sem, recv_sem=recv_sem, device_id=((me + 1) % SHARDS // 8, (me + 1) % SHARDS % 8),
        device_id_type=MESH)
    return own, every


def add_rows(count, target, sources):
    def step(index, carry):
        total = sources[0](index).astype(F32)
        for source in sources[1:]:
            total = total + source(index).astype(F32)
        target(index, total.astype(BF16))
        return carry

    lax.fori_loop(0, count, step, 0)


class Scatter:
    def __init__(self, at, slabs, buffers, sems, base, sums, which, scale):
        self.at, self.slabs, self.sums, self.which, self.scale = at, slabs, sums, which, scale
        self.from_core, self.first, self.second, self.third, *recvs = [
            buffers[i * COUNT:(i + 1) * COUNT] for i in range(7)]
        self.bufs, self.recvs = (self.first, self.second, self.third), recvs
        self.send_sem, self.recv_sem = sems
        self.base = base
        self.core, self.flying = {}, {}

    def copy(self, key, slot, src, dst, axis, step):
        slot = self.base + slot
        made = pltpu.make_async_remote_copy(
            src_ref=src, dst_ref=dst, send_sem=self.send_sem.at[slot], recv_sem=self.recv_sem.at[slot],
            device_id=device_of(moved(self.at, axis, step)), device_id_type=MESH)
        made.start()
        self.flying[key] = made

    def begin(self, part):
        self.copy((part, "core"), COUNT * 18 + part, self.slabs[part].at[:, :, 1 - self.at["core"]],
                  self.from_core[part], "core", 1)

    def join_cores(self, part):
        self.flying[(part, "core")].wait_recv()
        order, first = PARTS[part][3], self.first[part]
        mine, theirs, core = self.slabs[part], self.from_core[part], self.at["core"]

        def target(i, value):
            digit = {"x": (i % 2) * 2 + i // 32, "y": (i // 8) % 4, "z": (i // 2) % 4}
            first[digit[order[0]], digit[order[1]], digit[order[2]]] = value

        add_rows(64, target, [lambda i: mine[i // 32, (i // 8) % 4, core, (i // 2) % 4, i % 2],
                              lambda i: theirs[i // 32, (i // 8) % 4, (i // 2) % 4, i % 2]])
        self.start(part, 0)

    @staticmethod
    def halves(level, block):
        cut = 2 if level < 2 else 32
        return block.at[0:cut], block.at[cut:block.shape[0]]

    def start(self, part, level):
        axis = PARTS[part][3][level]
        here, source, recv = self.at[axis], self.bufs[level][part], self.recvs[level][part]
        for direction in (0, 1):
            step = 3 if direction else 1
            relay, plain = direction, 1 - direction
            far, near = source.at[(here + 2) % 4], source.at[(here + step) % 4]
            slot = ((part * 3 + level) * 2 + direction) * 3
            self.copy((part, level, direction, 0), slot, self.halves(level, far)[relay],
                      self.halves(level, recv.at[direction, 0])[relay], axis, step)
            self.copy((part, level, direction, 1), slot + 1, self.halves(level, near)[plain],
                      self.halves(level, recv.at[direction, 1])[plain], axis, step)

    def relay(self, part, level):
        axis = PARTS[part][3][level]
        here, source, recv = self.at[axis], self.bufs[level][part], self.recvs[level][part]
        for direction in (0, 1):
            step = 3 if direction else 1
            self.flying[(part, level, direction, 0)].wait_recv()
            near = self.halves(level, source.at[(here + step) % 4])[direction]
            came = self.halves(level, recv.at[direction, 0])[direction]
            if level == 0:
                def target(i, v):
                    came[i // 4, i % 4] = v
                add_rows(8, target, [lambda i: came[i // 4, i % 4], lambda i: near[i // 4, i % 4]])
            elif level == 1:
                def target(i, v):
                    came[i] = v
                add_rows(2, target, [lambda i: came[i], lambda i: near[i]])
            else:
                came[...] = (came[...].astype(F32) + near[...].astype(F32)).astype(BF16)
            slot = ((part * 3 + level) * 2 + direction) * 3 + 2
            self.copy((part, level, direction, 2), slot, came, self.halves(level, recv.at[direction, 1])[direction],
                      axis, step)

    def finish(self, part, level):
        axis = PARTS[part][3][level]
        source, recv = self.bufs[level][part].at[self.at[axis]], self.recvs[level][part]
        for direction in (0, 1):
            self.flying[(part, level, direction, 1)].wait_recv()
            self.flying[(part, level, direction, 2)].wait_recv()
        plus, minus = recv.at[0, 1], recv.at[1, 1]
        if level == 0:
            goal = self.second[part]

            def target(i, v):
                goal[i // 4, i % 4] = v
            add_rows(16, target, [lambda i: source[i // 4, i % 4], lambda i: plus[i // 4, i % 4],
                                  lambda i: minus[i // 4, i % 4]])
        elif level == 1:
            goal = self.third[part]

            def target(i, v):
                goal[i] = v
            add_rows(4, target, [lambda i: source[i], lambda i: plus[i], lambda i: minus[i]])
        else:
            start = sum(p[2] for p in PARTS[:part])
            self.sums[self.which, start:start + PARTS[part][2], :] = (
                source[...].astype(F32) + plus[...].astype(F32) + minus[...].astype(F32)) * self.scale
        if level < 2:
            self.start(part, level + 1)

    def drain_cores(self):
        for part in range(COUNT):
            self.flying.pop((part, "core")).wait_send()

    def drain(self):
        for made in self.flying.values():
            made.wait_send()


def parts_step(step, *level):
    for part in range(COUNT):
        step(part, *level)


def both_blocks(scale, clip_hbm, cot_hbm, wt_s_hbm, pt_s_hbm, adaln_s, gains_s, wt_t_hbm, pt_t_hbm, adaln_t, gains_t,
                result, grad_clip, sums,
                clip, cot, wt_s, pt_s, wt_t, pt_t, normed_s, normed_t, branch, qkv_s, qkv_t, mixed_f, dmixed_f,
                mixed_s, mixed_t, dqkv, left, work, tokens_a, tokens_b, send, recv_a, recv_b, slab0, slab1, slab2,
                *rest):
    buffers = rest[:7 * COUNT]
    load_sem, own_sem, send_a, send_b, got_a, got_b, sum_send, sum_recv, free_sem, core_free = rest[7 * COUNT:]
    at = place()
    me = lax.axis_index("wide") * 8 + lax.axis_index("narrow")
    loads = []
    for i, (hbm, vmem) in enumerate(((clip_hbm, clip), (wt_s_hbm, wt_s), (pt_s_hbm, pt_s), (cot_hbm, cot),
                                     (pt_t_hbm, pt_t), (wt_t_hbm, wt_t))):
        load = pltpu.make_async_copy(hbm, vmem, load_sem.at[i])
        load.start()
        loads.append(load)
    barrier = pltpu.get_barrier_semaphore()

    def greet(step, carry):
        other = (me + step) % SHARDS
        pl.semaphore_signal(barrier, inc=1, device_id=(other // 8, other % 8), device_id_type=MESH)
        return carry

    lax.fori_loop(1, SHARDS, greet, 0)

    loads[0].wait()
    norm_tokens(flat_rows(clip), adaln_s, normed_s)
    loads[1].wait()
    project_qkv(wt_s, normed_s, qkv_s)
    heads_loop(qkv_s, gains_s, mixed_f, None)
    wide_rows(mixed_f, HD, mixed_s)
    loads[2].wait()
    add_projection(flat_rows(clip), mixed_s, pt_s, adaln_s, functools.partial(put_tiles, tokens_a))
    pack_messages(tokens_a, send)
    pl.semaphore_wait(barrier, SHARDS - 1)
    own, every = start_exchange(me, send, recv_a, send_a, got_a, own_sem.at[0])

    loads[3].wait()
    gate_cotangent(flat_rows(cot), adaln_t, branch)
    loads[4].wait()
    pull_mixed(pt_t, branch, dmixed_f)
    loads[5].wait()
    own.wait()
    every.wait_recv()
    unpack_messages(recv_a, tokens_b)
    middle = tile_rows(tokens_b)
    norm_tokens(middle, adaln_t, normed_t)
    project_qkv(wt_t, normed_t, qkv_t)
    heads_loop(qkv_t, gains_t, mixed_f, dmixed_f)
    wide_rows(qkv_t, 3 * HD, dqkv)
    pull_norm(middle, flat_rows(cot), dqkv, wt_t, adaln_t, qkv_t, functools.partial(put_tiles, tokens_a))
    every.wait_send()
    pack_messages(tokens_a, send)
    own, every = start_exchange(me, send, recv_b, send_b, got_b, own_sem.at[1])
    wide_rows(mixed_f, HD, mixed_t)

    def put_result(rows, value):
        normed_t[rows, :] = value.astype(BF16)

    slabs = (slab0, slab1, slab2)
    sems = (sum_send, sum_recv)
    partner = device_of(moved(at, "core", 1))
    neighbours = [device_of(moved(at, a, d)) for a in ("x", "y", "z") for d in (1, 3)]
    sum_t = Scatter(at, slabs, buffers, sems, 0, sums, 1, scale)
    sum_s = Scatter(at, slabs, buffers, sems, COUNT * 19, sums, 0, scale)
    left[...] = normed_t[...].T
    for part in (0, 1):
        gradient_part(left, dqkv, PARTS[part][0], PARTS[part][1], slabs[part], work)
        sum_t.begin(part)
    left[...] = branch[...].T
    gradient_part(left, mixed_t, 0, PROJ_TILES, slabs[2], work)
    sum_t.begin(2)
    add_projection(middle, mixed_t, pt_t, adaln_t, put_result)
    store_result = pltpu.make_async_copy(normed_t, result, load_sem.at[6])
    store_result.start()
    parts_step(sum_t.join_cores)
    pl.semaphore_signal(core_free, inc=1, device_id=partner, device_id_type=MESH)

    own.wait()
    every.wait_recv()
    parts_step(sum_t.relay, 0)
    unpack_messages(recv_b, tokens_b)
    d_middle = tile_rows(tokens_b)
    gate_cotangent(d_middle, adaln_s, branch)
    pull_mixed(pt_s, branch, dmixed_f)
    parts_step(sum_t.finish, 0)
    left[...] = branch[...].T
    sum_t.drain_cores()
    pl.semaphore_wait(core_free, 1)
    gradient_part(left, mixed_s, 0, PROJ_TILES, slabs[2], work)
    sum_s.begin(2)
    parts_step(sum_t.relay, 1)
    heads_loop(qkv_s, gains_s, None, dmixed_f, 0, 1)
    parts_step(sum_t.finish, 1)
    heads_loop(qkv_s, gains_s, None, dmixed_f, 1, 2)
    parts_step(sum_t.relay, 2)

    def put_grad(rows, value):
        branch[rows, :] = value.astype(BF16)

    wide_rows(qkv_s, 3 * HD, dqkv)
    left[...] = normed_s[...].T
    gradient_part(left, dqkv, PARTS[0][0], PARTS[0][1], slabs[0], work)
    sum_s.begin(0)
    parts_step(sum_t.finish, 2)
    sum_t.drain()
    for peer in neighbours:
        pl.semaphore_signal(free_sem, inc=1, device_id=peer, device_id_type=MESH)
    gradient_part(left, dqkv, PARTS[1][0], PARTS[1][1], slabs[1], work)
    sum_s.begin(1)
    pl.semaphore_wait(free_sem, len(neighbours))
    sum_s.join_cores(2)
    sum_s.join_cores(0)
    sum_s.join_cores(1)
    pull_norm(flat_rows(clip), d_middle, dqkv, wt_s, adaln_s, qkv_s, put_grad)
    store_grad = pltpu.make_async_copy(branch, grad_clip, load_sem.at[7])
    store_grad.start()
    for level in range(3):
        parts_step(sum_s.relay, level)
        parts_step(sum_s.finish, level)
    sum_s.drain()
    every.wait_send()
    store_result.wait()
    store_grad.wait()


def split_sums(sums, qkv_s, proj_s, qkv_t, proj_t):
    for which, outs in enumerate(((qkv_s, proj_s), (qkv_t, proj_t))):
        start = 0
        for first, tiles, rows, _ in PARTS:
            out, base = (outs[0], 0) if first < QKV_TILES else (outs[1], QKV_TILES)
            for t in range(tiles):
                lane = (first + t - base) * 128
                width = min(128, out.shape[1] - lane)
                out[0:8, lane:lane + width] = sums[which, start + 8 * t:start + 8 * t + 8, :width]
                ninth = start + 8 * tiles + t
                out[8:9, lane:lane + width] = sums[which, ninth:ninth + 1, :width]
            start += rows


def run_blocks(scale, clip, cot, wt_s, pt_s, adaln_s, gains_s, wt_t, pt_t, adaln_t, gains_t):
    token, qkv_f, heads_f = ((TOKENS, MODEL), BF16), ((3 * HD, TOKENS), F32), ((HD, TOKENS), F32)
    tiles = ((LANE_TILES * TOKENS, 128), F32)
    mixed, message = ((TOKENS, PROJ_TILES * 128), BF16), ((SHARDS, MESSAGE, 128), BF16)
    shapes = [token, token, ((3 * HD, MODEL), BF16), ((HD, MODEL), BF16), ((3 * HD, MODEL), BF16), ((HD, MODEL), BF16),
              token, token, token, qkv_f, qkv_f, heads_f, heads_f, mixed, mixed, ((TOKENS, QKV_TILES * 128), BF16),
              ((MODEL, TOKENS), BF16), ((8 * MODEL, 128), F32), ((LANE_TILES * TOKENS + 8, 128), F32), tiles, message, message, message]
    shapes += [((2, 4, 2, 4, 2, rows, 128), BF16) for _, _, rows, _ in PARTS]
    for lead in ((2, 4, 4, 2), (4, 4, 4), (4, 4), (4,), (2, 2, 4, 4), (2, 2, 4), (2, 2)):
        shapes += [(lead + (rows, 128), BF16) for _, _, rows, _ in PARTS]
    vmem, hbm = pl.BlockSpec(memory_space=pltpu.VMEM), pl.BlockSpec(memory_space=pl.ANY)
    return pl.pallas_call(
        functools.partial(both_blocks, scale),
        out_shape=[jax.ShapeDtypeStruct(*token), jax.ShapeDtypeStruct(*token), jax.ShapeDtypeStruct((2, 176, 128), F32)],
        in_specs=[hbm, hbm, hbm, hbm, vmem, vmem, hbm, hbm, vmem, vmem],
        out_specs=[hbm, hbm, vmem],
        scratch_shapes=[pltpu.VMEM(*s) for s in shapes] + [
            pltpu.SemaphoreType.DMA((8,)), pltpu.SemaphoreType.DMA((2,)),
            pltpu.SemaphoreType.DMA, pltpu.SemaphoreType.DMA, pltpu.SemaphoreType.DMA, pltpu.SemaphoreType.DMA,
            pltpu.SemaphoreType.DMA((2 * COUNT * 19,)), pltpu.SemaphoreType.DMA((2 * COUNT * 19,)),
            pltpu.SemaphoreType.REGULAR, pltpu.SemaphoreType.REGULAR],
        compiler_params=pltpu.CompilerParams(collective_id=0, has_side_effects=True, vmem_limit_bytes=67043328),
        name="both_blocks",
    )(clip, cot, wt_s, pt_s, adaln_s, gains_s, wt_t, pt_t, adaln_t, gains_t)


def body(clip_tokens, cotangent, qkv_spatial, proj_spatial, adaln_spatial, qknorm_spatial,
         qkv_temporal, proj_temporal, adaln_temporal, qknorm_temporal):
    clip = clip_tokens.reshape(TOKENS, MODEL)
    cot = jnp.transpose(cotangent, (1, 0, 2)).reshape(TOKENS, MODEL)
    result, grad_clip, sums = run_blocks(
        1.0 / math.sqrt(SEQ * SEQ), clip, cot, qkv_spatial.T, proj_spatial.T, adaln_spatial, qknorm_spatial,
        qkv_temporal.T, proj_temporal.T, adaln_temporal, qknorm_temporal)
    grads = pl.pallas_call(
        split_sums,
        out_shape=[jax.ShapeDtypeStruct((9, 3 * HD), F32), jax.ShapeDtypeStruct((9, HD), F32)] * 2,
        in_specs=[pl.BlockSpec(memory_space=pltpu.VMEM)],
        out_specs=[pl.BlockSpec(memory_space=pltpu.VMEM)] * 4,
        name="split_sums",
    )(sums)
    result = jnp.transpose(result.reshape(2, SEQ, MODEL), (1, 0, 2))
    return (result, grad_clip.reshape(2, SEQ, MODEL), *grads)


def solution(mesh):
    in_specs = (
        P(("wide", "narrow"), None, None),
        P(None, ("wide", "narrow"), None),
        P(),
        P(),
        P(),
        P(),
        P(),
        P(),
        P(),
        P(),
    )
    out_specs = (
        P(None, ("wide", "narrow"), None),
        P(("wide", "narrow"), None, None),
        P(("wide", "narrow"), None),
        P(("wide", "narrow"), None),
        P(("wide", "narrow"), None),
        P(("wide", "narrow"), None),
    )
    return jax.shard_map(body, mesh=mesh, in_specs=in_specs, out_specs=out_specs, check_vma=False)
```

```python
import functools
import math

import jax
import jax.numpy as jnp
from jax import lax
from jax.experimental import pallas as pl
from jax.experimental.pallas import tpu as pltpu
from jax.sharding import PartitionSpec as P

HDIM = 72
HEADS = 8
HD = HDIM * HEADS
MODEL = 1152
LANE_TILES = MODEL // 128
TOKENS = 512
SEQ = 256
EPSILON = 1e-06
QKV_TILES, PROJ_TILES = 14, 5
SHARDS = 128
MESSAGE = 40
NT = (((1,), (1,)), ((), ()))
TN = (((0,), (0,)), ((), ()))
F32, BF16 = jnp.float32, jnp.bfloat16
MESH = pl.DeviceIdType.MESH
PARTS = ((0, 7, 64, ("y", "z", "x")), (7, 7, 64, ("z", "x", "y")), (14, 5, 48, ("x", "y", "z")))
COUNT = len(PARTS)


def place():
    wide = lax.axis_index("wide")
    narrow = lax.axis_index("narrow")
    x_lo, y, core = wide // 8, (wide // 2) % 4, wide % 2
    z, x_hi = narrow // 2, narrow % 2
    return {"x": x_hi * 2 + x_lo, "y": y, "z": z, "core": core}


def device_of(at):
    wide = (at["x"] % 2) * 8 + at["y"] * 2 + at["core"]
    narrow = at["z"] * 2 + at["x"] // 2
    return (wide, narrow)


def moved(at, axis, step):
    size = 2 if axis == "core" else 4
    return {**at, axis: (at[axis] + step) % size}


def row_loop(total, step, body, unroll=1):
    lax.fori_loop(0, total // step, lambda i, c: (body(pl.ds(pl.multiple_of(i * step, step), step)), c)[1], 0,
                  unroll=unroll)


def flat_rows(ref):
    return lambda rows: ref[rows, :].astype(F32)


def tile_rows(ref):
    return lambda rows: jnp.concatenate(
        [ref[pl.ds(pl.multiple_of(t * TOKENS + rows.start, 8), rows.size), :] for t in range(LANE_TILES)], axis=1)


def put_tiles(ref, rows, value):
    for t in range(LANE_TILES):
        ref[pl.ds(pl.multiple_of(t * TOKENS + rows.start, 8), rows.size), :] = value[:, t * 128:t * 128 + 128]


def centred(x):
    centre = x - jnp.mean(x, axis=-1, keepdims=True)
    spread = jnp.mean(centre * centre, axis=-1, keepdims=True)
    scale = lax.rsqrt(spread + EPSILON)
    return centre * scale, scale


def norm_tokens(x, adaln, normed):
    def body(rows):
        hat, _ = centred(x(rows))
        normed[rows, :] = (hat * (1.0 + adaln[1:2, :]) + adaln[0:1, :]).astype(BF16)

    row_loop(TOKENS, 16, body, 4)


def project_qkv(weight_t, normed, qkv_t):
    def body(i, carry):
        rows = pl.ds(pl.multiple_of(i * 576, 64), 576)
        qkv_t[rows, :] = lax.dot_general(weight_t[rows, :], normed[...], NT, preferred_element_type=F32)
        return carry

    lax.fori_loop(0, 3, body, 0)


def gate_cotangent(cot, adaln, branch):
    def body(rows):
        branch[rows, :] = (adaln[2:3, :] * cot(rows)).astype(BF16)

    row_loop(TOKENS, 64, body)


def pull_mixed(proj_t, branch, dmixed_t):
    dmixed_t[...] = lax.dot_general(proj_t[...], branch[...], NT, preferred_element_type=F32)


def column(row):
    grid = (HDIM, HDIM)
    same = lax.broadcasted_iota(jnp.int32, grid, 0) == lax.broadcasted_iota(jnp.int32, grid, 1)
    return jnp.sum(jnp.where(same, jnp.broadcast_to(row, grid), 0.0), axis=1, keepdims=True)


def split3(value):
    high = value.astype(BF16).astype(F32)
    return high, value - high


def heads_loop(qkv_t, gains, mixed_t, dmixed_t, first=0, last=2, unroll=1):
    root = 1.0 / math.sqrt(HDIM)
    q_gain, k_gain = column(gains[0:1, :]), column(gains[1:2, :])

    def one(head, seq):
        lanes = pl.ds(pl.multiple_of(seq * SEQ, SEQ), SEQ)
        at = [pl.ds(pl.multiple_of(part * HD + head * HDIM, 8), HDIM) for part in range(3)]
        loaded = [qkv_t[rows, lanes] for rows in at]
        loaded.append(None if dmixed_t is None else dmixed_t[at[0], lanes])
        return at, lanes, loaded

    def compute(at, lanes, loaded):
        q, k, v, d_mixed = loaded
        stores = []
        q_scale = lax.rsqrt(jnp.mean(q * q, axis=0, keepdims=True) + EPSILON)
        k_scale = lax.rsqrt(jnp.mean(k * k, axis=0, keepdims=True) + EPSILON)
        q_hat, k_hat = q * q_scale, k * k_scale
        qs, kn = q_hat * (q_gain * root), k_hat * k_gain
        q_high, q_low = split3(qs)
        k_high, k_low = split3(kn)
        q3 = jnp.concatenate([q_high, q_low, q_high], axis=0).astype(BF16)
        k3 = jnp.concatenate([k_high, k_high, k_low], axis=0).astype(BF16)
        raised = jnp.exp(lax.dot_general(k3, q3, TN, preferred_element_type=F32))
        inverse = 1.0 / jnp.sum(raised, axis=0, keepdims=True)
        v_low = v.astype(BF16)
        if mixed_t is not None:
            out = jnp.dot(v_low, raised.astype(BF16), preferred_element_type=F32) * inverse
            stores.append((mixed_t, at[0], out))
        if dmixed_t is not None:
            weights = raised * inverse
            d_out = d_mixed.astype(BF16)
            d_weights = lax.dot_general(v_low, d_out, TN, preferred_element_type=F32)
            shift = jnp.sum(weights * d_weights, axis=0, keepdims=True)
            d_scores = (weights * (d_weights - shift)).astype(BF16)
            dv = jnp.dot(weights.astype(BF16), d_out.T, preferred_element_type=F32).T
            dq = jnp.dot(k_high.astype(BF16), d_scores, preferred_element_type=F32)
            dk = jnp.dot(d_scores, q_high.astype(BF16).T, preferred_element_type=F32).T
            dq = dq * (q_gain * root)
            dk = dk * k_gain
            stores.append((qkv_t, at[0], q_scale * (dq - q_hat * jnp.mean(q_hat * dq, axis=0, keepdims=True))))
            stores.append((qkv_t, at[1], k_scale * (dk - k_hat * jnp.mean(k_hat * dk, axis=0, keepdims=True))))
            stores.append((qkv_t, at[2], dv))
        return lanes, stores

    def body(index, carry):
        taken = [one(index * 4 + i // 2, i % 2) for i in range(8)]
        for lanes, stores in [compute(*t) for t in taken]:
            for ref, rows, value in stores:
                ref[rows, lanes] = value
        return carry

    lax.fori_loop(first, last, body, 0, unroll=unroll)


def wide_rows(source, used, ref):
    ref[:, :used] = source[...].T.astype(BF16)
    ref[:, used:] = jnp.zeros((TOKENS, ref.shape[1] - used), BF16)


def add_projection(x, mixed, proj_t, adaln, put):
    def body(rows):
        projected = jnp.dot(mixed[rows, :HD], proj_t[...], preferred_element_type=F32)
        put(rows, x(rows) + adaln[2:3, :] * projected)

    row_loop(TOKENS, 256, body)


def pull_norm(x, cot, dqkv, weight_t, adaln, work, put):
    third = MODEL // 3
    for i in range(3):
        work[i * TOKENS:(i + 1) * TOKENS, :third] = jnp.dot(
            dqkv[:, :3 * HD], weight_t[:, i * third:(i + 1) * third], preferred_element_type=F32)

    def body(rows):
        d_normed = jnp.concatenate(
            [work[pl.ds(pl.multiple_of(i * TOKENS + rows.start, 8), rows.size), :third] for i in range(3)], axis=1)
        hat, scale = centred(x(rows))
        u = d_normed * (1.0 + adaln[1:2, :])
        d_x = scale * (u - jnp.mean(u, axis=-1, keepdims=True) - hat * jnp.mean(u * hat, axis=-1, keepdims=True))
        put(rows, cot(rows) + d_x)

    row_loop(TOKENS, 16, body, 4)


def gradient_part(left, right, first_tile, tiles, slab, work):
    done = 0
    while done < tiles:
        size = min(2, tiles - done)
        lane = pl.multiple_of((first_tile + done) * 128, 128)
        out = jnp.dot(left[...], right[:, pl.ds(lane, size * 128)], preferred_element_type=F32)
        for t in range(size):
            work[(done + t) * MODEL:(done + t + 1) * MODEL, :] = out[:, t * 128:(t + 1) * 128]
        done += size

    pad = slab.shape[-2] - 8 * tiles - 8

    def gather(wide, carry):
        goal, base = slab.at[wide // 8, (wide // 2) % 4, wide % 2], pl.multiple_of(wide * 72, 8)
        for narrow in range(8):
            at = base + 9 * narrow
            rows = [work[pl.ds(t * MODEL + at, 8), :] for t in range(tiles)]
            rows.append(work[pl.ds(at + 8, 8, stride=MODEL), :])
            if pad:
                rows.append(jnp.zeros((pad, 128), F32))
            goal[narrow // 2, narrow % 2] = jnp.concatenate(rows, axis=0).astype(BF16)
        return carry

    lax.fori_loop(0, SHARDS // 8, gather, 0)


def split_pairs(pairs, tokens):
    def body(rows):
        for which in range(2):
            tokens[pl.ds(pl.multiple_of(which * SEQ + rows.start, 16), 16), :] = pairs[rows, which, :]

    row_loop(SEQ, 16, body)


def join_pairs(tokens, pairs):
    def body(rows):
        for which in range(2):
            pairs[rows, which, :] = tokens[pl.ds(pl.multiple_of(which * SEQ + rows.start, 16), 16), :]

    row_loop(SEQ, 16, body)


def pack_messages(source, send):
    top = lax.broadcasted_iota(jnp.int32, (8, 128), 0) < 2

    def body(s, carry):
        rows = [source[pl.ds(a * SEQ + 2 * s + b, 8, stride=TOKENS), :] for a in range(2) for b in range(2)]
        last = 8 * TOKENS + 2 * s
        rows.append(jnp.where(top, source[pl.ds(last, 8), :], source[pl.ds(last + SEQ - 2, 8), :]))
        send[s] = jnp.concatenate(rows, axis=0).astype(BF16)
        return carry

    lax.fori_loop(0, SHARDS, body, 0, unroll=4)


def unpack_messages(recv, target):
    def body(s, carry):
        rows = recv[s].astype(F32)
        for a in range(2):
            for b in range(2):
                at = (a * 2 + b) * 8
                target[pl.ds(b * SEQ + 2 * s + a, 8, stride=TOKENS), :] = rows[at:at + 8]
            target[pl.ds(8 * TOKENS + 2 * s + a, 2, stride=SEQ), :] = rows[32 + 2 * a:34 + 2 * a]
        return carry

    lax.fori_loop(0, SHARDS, body, 0, unroll=4)


def start_exchange(me, send, recv, send_sem, recv_sem, own_sem):
    def body(step, carry):
        other = (me + step * 37) % SHARDS
        pltpu.make_async_remote_copy(
            src_ref=send.at[other], dst_ref=recv.at[me], send_sem=send_sem, recv_sem=recv_sem,
            device_id=(other // 8, other % 8), device_id_type=MESH).start()
        return carry

    lax.fori_loop(1, SHARDS, body, 0)
    own = pltpu.make_async_copy(send.at[me], recv.at[me], own_sem)
    own.start()
    every = pltpu.make_async_remote_copy(
        src_ref=send.at[pl.ds(0, SHARDS - 1)], dst_ref=recv.at[pl.ds(0, SHARDS - 1)],
        send_sem=send_sem, recv_sem=recv_sem, device_id=((me + 1) % SHARDS // 8, (me + 1) % SHARDS % 8),
        device_id_type=MESH)
    return own, every


def add_rows(count, target, sources):
    def step(index, carry):
        total = sources[0](index).astype(F32)
        for source in sources[1:]:
            total = total + source(index).astype(F32)
        target(index, total.astype(BF16))
        return carry

    lax.fori_loop(0, count, step, 0)


class Scatter:
    def __init__(self, at, slabs, buffers, sems, base, sums, which, scale):
        self.at, self.slabs, self.sums, self.which, self.scale = at, slabs, sums, which, scale
        self.from_core, self.first, self.second, self.third, *recvs = [
            buffers[i * COUNT:(i + 1) * COUNT] for i in range(7)]
        self.bufs, self.recvs = (self.first, self.second, self.third), recvs
        self.send_sem, self.recv_sem = sems
        self.base = base
        self.core, self.flying = {}, {}

    def copy(self, key, slot, src, dst, axis, step):
        slot = self.base + slot
        made = pltpu.make_async_remote_copy(
            src_ref=src, dst_ref=dst, send_sem=self.send_sem.at[slot], recv_sem=self.recv_sem.at[slot],
            device_id=device_of(moved(self.at, axis, step)), device_id_type=MESH)
        made.start()
        self.flying[key] = made

    def begin(self, part):
        self.copy((part, "core"), COUNT * 18 + part, self.slabs[part].at[:, :, 1 - self.at["core"]],
                  self.from_core[part], "core", 1)

    def join_cores(self, part):
        self.flying[(part, "core")].wait_recv()
        order, first = PARTS[part][3], self.first[part]
        mine, theirs, core = self.slabs[part], self.from_core[part], self.at["core"]

        def target(i, value):
            digit = {"x": (i % 2) * 2 + i // 32, "y": (i // 8) % 4, "z": (i // 2) % 4}
            first[digit[order[0]], digit[order[1]], digit[order[2]]] = value

        add_rows(64, target, [lambda i: mine[i // 32, (i // 8) % 4, core, (i // 2) % 4, i % 2],
                              lambda i: theirs[i // 32, (i // 8) % 4, (i // 2) % 4, i % 2]])
        self.start(part, 0)

    @staticmethod
    def halves(level, block):
        cut = 2 if level < 2 else 32
        return block.at[0:cut], block.at[cut:block.shape[0]]

    def start(self, part, level):
        axis = PARTS[part][3][level]
        here, source, recv = self.at[axis], self.bufs[level][part], self.recvs[level][part]
        for direction in (0, 1):
            step = 3 if direction else 1
            relay, plain = direction, 1 - direction
            far, near = source.at[(here + 2) % 4], source.at[(here + step) % 4]
            slot = ((part * 3 + level) * 2 + direction) * 3
            self.copy((part, level, direction, 0), slot, self.halves(level, far)[relay],
                      self.halves(level, recv.at[direction, 0])[relay], axis, step)
            self.copy((part, level, direction, 1), slot + 1, self.halves(level, near)[plain],
                      self.halves(level, recv.at[direction, 1])[plain], axis, step)

    def relay(self, part, level):
        axis = PARTS[part][3][level]
        here, source, recv = self.at[axis], self.bufs[level][part], self.recvs[level][part]
        for direction in (0, 1):
            step = 3 if direction else 1
            self.flying[(part, level, direction, 0)].wait_recv()
            near = self.halves(level, source.at[(here + step) % 4])[direction]
            came = self.halves(level, recv.at[direction, 0])[direction]
            if level == 0:
                def target(i, v):
                    came[i // 4, i % 4] = v
                add_rows(8, target, [lambda i: came[i // 4, i % 4], lambda i: near[i // 4, i % 4]])
            elif level == 1:
                def target(i, v):
                    came[i] = v
                add_rows(2, target, [lambda i: came[i], lambda i: near[i]])
            else:
                came[...] = (came[...].astype(F32) + near[...].astype(F32)).astype(BF16)
            slot = ((part * 3 + level) * 2 + direction) * 3 + 2
            self.copy((part, level, direction, 2), slot, came, self.halves(level, recv.at[direction, 1])[direction],
                      axis, step)

    def finish(self, part, level):
        axis = PARTS[part][3][level]
        source, recv = self.bufs[level][part].at[self.at[axis]], self.recvs[level][part]
        for direction in (0, 1):
            self.flying[(part, level, direction, 1)].wait_recv()
            self.flying[(part, level, direction, 2)].wait_recv()
        plus, minus = recv.at[0, 1], recv.at[1, 1]
        if level == 0:
            goal = self.second[part]

            def target(i, v):
                goal[i // 4, i % 4] = v
            add_rows(16, target, [lambda i: source[i // 4, i % 4], lambda i: plus[i // 4, i % 4],
                                  lambda i: minus[i // 4, i % 4]])
        elif level == 1:
            goal = self.third[part]

            def target(i, v):
                goal[i] = v
            add_rows(4, target, [lambda i: source[i], lambda i: plus[i], lambda i: minus[i]])
        else:
            start = sum(p[2] for p in PARTS[:part])
            self.sums[self.which, start:start + PARTS[part][2], :] = (
                source[...].astype(F32) + plus[...].astype(F32) + minus[...].astype(F32)) * self.scale

    def drain_cores(self):
        for part in range(COUNT):
            self.flying.pop((part, "core")).wait_send()

    def release(self, level, neighbours, free):
        for part in range(COUNT):
            for direction in (0, 1):
                for kind in range(3):
                    self.flying.pop((part, level, direction, kind)).wait_send()
        for peer in neighbours:
            pl.semaphore_signal(free.at[level], inc=1, device_id=peer, device_id_type=MESH)

    def drain(self):
        for made in self.flying.values():
            made.wait_send()


def parts_step(step, *level):
    for part in range(COUNT):
        step(part, *level)


def next_level(scatter, level):
    for part in range(COUNT):
        scatter.finish(part, level)
        scatter.start(part, level + 1)


def both_blocks(scale, clip_hbm, cot_hbm, wt_s_hbm, pt_s_hbm, adaln_s, gains_s, wt_t_hbm, pt_t_hbm, adaln_t, gains_t,
                result, grad_clip, sums,
                clip, pairs, cot, wt_s, pt_s, wt_t, pt_t, normed_s, normed_t, branch, qkv_s, qkv_t, mixed_f, dmixed_f,
                mixed_s, mixed_t, dqkv, left, work, tokens_b, send, recv_a, recv_b, slab0, slab1, slab2,
                *rest):
    buffers = rest[:7 * COUNT]
    load_sem, own_sem, send_a, send_b, got_a, got_b, sum_send, sum_recv, free_sem, core_free = rest[7 * COUNT:]
    at = place()
    me = lax.axis_index("wide") * 8 + lax.axis_index("narrow")
    loads = []
    for i, (hbm, vmem) in enumerate(((clip_hbm, clip), (wt_s_hbm, wt_s), (pt_s_hbm, pt_s), (cot_hbm, pairs),
                                     (pt_t_hbm, pt_t), (wt_t_hbm, wt_t))):
        load = pltpu.make_async_copy(hbm, vmem, load_sem.at[i])
        load.start()
        loads.append(load)
    barrier = pltpu.get_barrier_semaphore()

    def greet(step, carry):
        other = (me + step) % SHARDS
        pl.semaphore_signal(barrier, inc=1, device_id=(other // 8, other % 8), device_id_type=MESH)
        return carry

    lax.fori_loop(1, SHARDS, greet, 0)

    loads[0].wait()
    norm_tokens(flat_rows(clip), adaln_s, normed_s)
    loads[1].wait()
    project_qkv(wt_s, normed_s, qkv_s)
    heads_loop(qkv_s, gains_s, mixed_f, None)
    wide_rows(mixed_f, HD, mixed_s)
    loads[2].wait()
    add_projection(flat_rows(clip), mixed_s, pt_s, adaln_s, functools.partial(put_tiles, work))
    pack_messages(work, send)
    pl.semaphore_wait(barrier, SHARDS - 1)
    own, every = start_exchange(me, send, recv_a, send_a, got_a, own_sem.at[0])

    loads[3].wait()
    split_pairs(pairs, cot)
    gate_cotangent(flat_rows(cot), adaln_t, branch)
    loads[4].wait()
    pull_mixed(pt_t, branch, dmixed_f)
    loads[5].wait()
    own.wait()
    every.wait_recv()
    unpack_messages(recv_a, tokens_b)
    middle = tile_rows(tokens_b)
    norm_tokens(middle, adaln_t, normed_t)
    project_qkv(wt_t, normed_t, qkv_t)
    heads_loop(qkv_t, gains_t, mixed_f, dmixed_f)
    wide_rows(qkv_t, 3 * HD, dqkv)
    pull_norm(middle, flat_rows(cot), dqkv, wt_t, adaln_t, qkv_t, functools.partial(put_tiles, work))
    every.wait_send()
    pack_messages(work, send)
    own, every = start_exchange(me, send, recv_b, send_b, got_b, own_sem.at[1])
    wide_rows(mixed_f, HD, mixed_t)

    def put_result(rows, value):
        normed_t[rows, :] = value.astype(BF16)

    slabs = (slab0, slab1, slab2)
    sems = (sum_send, sum_recv)
    partner = device_of(moved(at, "core", 1))
    neighbours = [device_of(moved(at, a, d)) for a in ("x", "y", "z") for d in (1, 3)]
    sum_t = Scatter(at, slabs, buffers, sems, 0, sums, 1, scale)
    sum_s = Scatter(at, slabs, buffers, sems, COUNT * 19, sums, 0, scale)
    left[...] = normed_t[...].T
    for part in (0, 1):
        gradient_part(left, dqkv, PARTS[part][0], PARTS[part][1], slabs[part], work)
        sum_t.begin(part)
    left[...] = branch[...].T
    gradient_part(left, mixed_t, 0, PROJ_TILES, slabs[2], work)
    sum_t.begin(2)
    add_projection(middle, mixed_t, pt_t, adaln_t, put_result)
    join_pairs(normed_t, pairs)
    store_result = pltpu.make_async_copy(pairs, result, load_sem.at[6])
    store_result.start()

    own.wait()
    every.wait_recv()
    parts_step(sum_t.join_cores)
    pl.semaphore_signal(core_free, inc=1, device_id=partner, device_id_type=MESH)
    unpack_messages(recv_b, tokens_b)
    d_middle = tile_rows(tokens_b)
    gate_cotangent(d_middle, adaln_s, branch)
    pull_mixed(pt_s, branch, dmixed_f)
    left[...] = branch[...].T
    sum_t.drain_cores()
    pl.semaphore_wait(core_free, 1)
    gradient_part(left, mixed_s, 0, PROJ_TILES, slabs[2], work)
    sum_s.begin(2)
    parts_step(sum_t.relay, 0)
    heads_loop(qkv_s, gains_s, None, dmixed_f)
    next_level(sum_t, 0)
    sum_t.release(0, neighbours, free_sem)

    def put_grad(rows, value):
        branch[rows, :] = value.astype(BF16)

    wide_rows(qkv_s, 3 * HD, dqkv)
    left[...] = normed_s[...].T
    gradient_part(left, dqkv, PARTS[0][0], PARTS[0][1], slabs[0], work)
    sum_s.begin(0)
    parts_step(sum_t.relay, 1)
    gradient_part(left, dqkv, PARTS[1][0], PARTS[1][1], slabs[1], work)
    sum_s.begin(1)
    pl.semaphore_wait(free_sem.at[0], len(neighbours))
    for part in (2, 0, 1):
        sum_s.join_cores(part)
    next_level(sum_t, 1)
    sum_t.release(1, neighbours, free_sem)
    pull_norm(flat_rows(clip), d_middle, dqkv, wt_s, adaln_s, qkv_s, put_grad)
    store_grad = pltpu.make_async_copy(branch, grad_clip, load_sem.at[7])
    store_grad.start()
    parts_step(sum_t.relay, 2)
    parts_step(sum_s.relay, 0)
    parts_step(sum_t.finish, 2)
    sum_t.release(2, neighbours, free_sem)
    pl.semaphore_wait(free_sem.at[1], len(neighbours))
    next_level(sum_s, 0)
    parts_step(sum_s.relay, 1)
    pl.semaphore_wait(free_sem.at[2], len(neighbours))
    next_level(sum_s, 1)
    parts_step(sum_s.relay, 2)
    parts_step(sum_s.finish, 2)
    sum_s.drain()
    every.wait_send()
    store_result.wait()
    store_grad.wait()


def split_sums(sums, qkv_s, proj_s, qkv_t, proj_t):
    for which, outs in enumerate(((qkv_s, proj_s), (qkv_t, proj_t))):
        start = 0
        for first, tiles, rows, _ in PARTS:
            out, base = (outs[0], 0) if first < QKV_TILES else (outs[1], QKV_TILES)
            for t in range(tiles):
                lane = (first + t - base) * 128
                width = min(128, out.shape[1] - lane)
                out[0:8, lane:lane + width] = sums[which, start + 8 * t:start + 8 * t + 8, :width]
                ninth = start + 8 * tiles + t
                out[8:9, lane:lane + width] = sums[which, ninth:ninth + 1, :width]
            start += rows


def run_blocks(scale, clip, cot, wt_s, pt_s, adaln_s, gains_s, wt_t, pt_t, adaln_t, gains_t):
    token, qkv_f, heads_f = ((TOKENS, MODEL), BF16), ((3 * HD, TOKENS), F32), ((HD, TOKENS), F32)
    tiles = ((LANE_TILES * TOKENS, 128), F32)
    mixed, message = ((TOKENS, PROJ_TILES * 128), BF16), ((SHARDS, MESSAGE, 128), BF16)
    pairs = ((SEQ, 2, MODEL), BF16)
    shapes = [token, pairs, token, ((3 * HD, MODEL), BF16), ((HD, MODEL), BF16), ((3 * HD, MODEL), BF16), ((HD, MODEL), BF16),
              token, token, token, qkv_f, qkv_f, heads_f, heads_f, mixed, mixed, ((TOKENS, QKV_TILES * 128), BF16),
              ((MODEL, TOKENS), BF16), ((8 * MODEL, 128), F32), tiles, message, message, message]
    shapes += [((2, 4, 2, 4, 2, rows, 128), BF16) for _, _, rows, _ in PARTS]
    for lead in ((2, 4, 4, 2), (4, 4, 4), (4, 4), (4,), (2, 2, 4, 4), (2, 2, 4), (2, 2)):
        shapes += [(lead + (rows, 128), BF16) for _, _, rows, _ in PARTS]
    vmem, hbm = pl.BlockSpec(memory_space=pltpu.VMEM), pl.BlockSpec(memory_space=pl.ANY)
    return pl.pallas_call(
        functools.partial(both_blocks, scale),
        out_shape=[jax.ShapeDtypeStruct(*pairs), jax.ShapeDtypeStruct(*token), jax.ShapeDtypeStruct((2, 176, 128), F32)],
        in_specs=[hbm, hbm, hbm, hbm, vmem, vmem, hbm, hbm, vmem, vmem],
        out_specs=[hbm, hbm, vmem],
        scratch_shapes=[pltpu.VMEM(*s) for s in shapes] + [
            pltpu.SemaphoreType.DMA((8,)), pltpu.SemaphoreType.DMA((2,)),
            pltpu.SemaphoreType.DMA, pltpu.SemaphoreType.DMA, pltpu.SemaphoreType.DMA, pltpu.SemaphoreType.DMA,
            pltpu.SemaphoreType.DMA((2 * COUNT * 19,)), pltpu.SemaphoreType.DMA((2 * COUNT * 19,)),
            pltpu.SemaphoreType.REGULAR((3,)), pltpu.SemaphoreType.REGULAR],
        compiler_params=pltpu.CompilerParams(collective_id=0, has_side_effects=True, vmem_limit_bytes=67043328),
        name="both_blocks",
    )(clip, cot, wt_s, pt_s, adaln_s, gains_s, wt_t, pt_t, adaln_t, gains_t)


def body(clip_tokens, cotangent, qkv_spatial, proj_spatial, adaln_spatial, qknorm_spatial,
         qkv_temporal, proj_temporal, adaln_temporal, qknorm_temporal):
    clip = clip_tokens.reshape(TOKENS, MODEL)
    result, grad_clip, sums = run_blocks(
        1.0 / math.sqrt(SEQ * SEQ), clip, cotangent, qkv_spatial.T, proj_spatial.T, adaln_spatial, qknorm_spatial,
        qkv_temporal.T, proj_temporal.T, adaln_temporal, qknorm_temporal)
    grads = pl.pallas_call(
        split_sums,
        out_shape=[jax.ShapeDtypeStruct((9, 3 * HD), F32), jax.ShapeDtypeStruct((9, HD), F32)] * 2,
        in_specs=[pl.BlockSpec(memory_space=pltpu.VMEM)],
        out_specs=[pl.BlockSpec(memory_space=pltpu.VMEM)] * 4,
        name="split_sums",
    )(sums)
    return (result, grad_clip.reshape(2, SEQ, MODEL), *grads)


def solution(mesh):
    in_specs = (
        P(("wide", "narrow"), None, None),
        P(None, ("wide", "narrow"), None),
        P(),
        P(),
        P(),
        P(),
        P(),
        P(),
        P(),
        P(),
    )
    out_specs = (
        P(None, ("wide", "narrow"), None),
        P(("wide", "narrow"), None, None),
        P(("wide", "narrow"), None),
        P(("wide", "narrow"), None),
        P(("wide", "narrow"), None),
        P(("wide", "narrow"), None),
    )
    return jax.shard_map(body, mesh=mesh, in_specs=in_specs, out_specs=out_specs, check_vma=False)
```

```python
import functools
import math

import jax
import jax.numpy as jnp
from jax import lax
from jax.experimental import pallas as pl
from jax.experimental.pallas import tpu as pltpu
from jax.sharding import PartitionSpec as P

HDIM = 72
HEADS = 8
HD = HDIM * HEADS
MODEL = 1152
LANE_TILES = MODEL // 128
TOKENS = 512
SEQ = 256
EPSILON = 1e-06
QKV_TILES, PROJ_TILES = 14, 5
SHARDS = 128
MESSAGE = 40
NT = (((1,), (1,)), ((), ()))
TN = (((0,), (0,)), ((), ()))
F32, BF16 = jnp.float32, jnp.bfloat16
MESH = pl.DeviceIdType.MESH
PARTS = ((0, 7, 64, ("y", "z", "x")), (7, 7, 64, ("z", "x", "y")), (14, 5, 48, ("x", "y", "z")))
COUNT = len(PARTS)


def place():
    wide = lax.axis_index("wide")
    narrow = lax.axis_index("narrow")
    x_lo, y, core = wide // 8, (wide // 2) % 4, wide % 2
    z, x_hi = narrow // 2, narrow % 2
    return {"x": x_hi * 2 + x_lo, "y": y, "z": z, "core": core}


def device_of(at):
    wide = (at["x"] % 2) * 8 + at["y"] * 2 + at["core"]
    narrow = at["z"] * 2 + at["x"] // 2
    return (wide, narrow)


def moved(at, axis, step):
    size = 2 if axis == "core" else 4
    return {**at, axis: (at[axis] + step) % size}


def row_loop(total, step, body, unroll=1):
    lax.fori_loop(0, total // step, lambda i, c: (body(pl.ds(pl.multiple_of(i * step, step), step)), c)[1], 0,
                  unroll=unroll)


def flat_rows(ref):
    return lambda rows: ref[rows, :].astype(F32)


def tile_rows(ref):
    return lambda rows: jnp.concatenate(
        [ref[pl.ds(pl.multiple_of(t * TOKENS + rows.start, 8), rows.size), :] for t in range(LANE_TILES)], axis=1)


def put_tiles(ref, rows, value):
    for t in range(LANE_TILES):
        ref[pl.ds(pl.multiple_of(t * TOKENS + rows.start, 8), rows.size), :] = value[:, t * 128:t * 128 + 128]


def centred(x):
    centre = x - jnp.mean(x, axis=-1, keepdims=True)
    spread = jnp.mean(centre * centre, axis=-1, keepdims=True)
    scale = lax.rsqrt(spread + EPSILON)
    return centre * scale, scale


def norm_tokens(x, adaln, normed):
    def body(rows):
        hat, _ = centred(x(rows))
        normed[rows, :] = (hat * (1.0 + adaln[1:2, :]) + adaln[0:1, :]).astype(BF16)

    row_loop(TOKENS, 16, body, 4)


def project_qkv(weight_t, normed, qkv_t):
    def body(i, carry):
        rows = pl.ds(pl.multiple_of(i * 576, 64), 576)
        qkv_t[rows, :] = lax.dot_general(weight_t[rows, :], normed[...], NT, preferred_element_type=F32)
        return carry

    lax.fori_loop(0, 3, body, 0)


def gate_cotangent(cot, adaln, branch):
    def body(rows):
        branch[rows, :] = (adaln[2:3, :] * cot(rows)).astype(BF16)

    row_loop(TOKENS, 64, body)


def pull_mixed(proj_t, branch, dmixed_t):
    dmixed_t[...] = lax.dot_general(proj_t[...], branch[...], NT, preferred_element_type=F32)


def column(row):
    grid = (HDIM, HDIM)
    same = lax.broadcasted_iota(jnp.int32, grid, 0) == lax.broadcasted_iota(jnp.int32, grid, 1)
    return jnp.sum(jnp.where(same, jnp.broadcast_to(row, grid), 0.0), axis=1, keepdims=True)


def split3(value):
    high = value.astype(BF16).astype(F32)
    return high, value - high


def heads_loop(qkv_t, gains, mixed_t, dmixed_t, first=0, last=2, unroll=1):
    root = 1.0 / math.sqrt(HDIM)
    q_gain, k_gain = column(gains[0:1, :]), column(gains[1:2, :])

    def one(head, seq):
        lanes = pl.ds(pl.multiple_of(seq * SEQ, SEQ), SEQ)
        at = [pl.ds(pl.multiple_of(part * HD + head * HDIM, 8), HDIM) for part in range(3)]
        loaded = [qkv_t[rows, lanes] for rows in at]
        loaded.append(None if dmixed_t is None else dmixed_t[at[0], lanes])
        return at, lanes, loaded

    def compute(at, lanes, loaded):
        q, k, v, d_mixed = loaded
        stores = []
        q_scale = lax.rsqrt(jnp.mean(q * q, axis=0, keepdims=True) + EPSILON)
        k_scale = lax.rsqrt(jnp.mean(k * k, axis=0, keepdims=True) + EPSILON)
        q_hat, k_hat = q * q_scale, k * k_scale
        qs, kn = q_hat * (q_gain * root), k_hat * k_gain
        q_high, q_low = split3(qs)
        k_high, k_low = split3(kn)
        q3 = jnp.concatenate([q_high, q_low, q_high], axis=0).astype(BF16)
        k3 = jnp.concatenate([k_high, k_high, k_low], axis=0).astype(BF16)
        raised = jnp.exp(lax.dot_general(k3, q3, TN, preferred_element_type=F32))
        inverse = 1.0 / jnp.sum(raised, axis=0, keepdims=True)
        v_low = v.astype(BF16)
        if mixed_t is not None:
            out = jnp.dot(v_low, raised.astype(BF16), preferred_element_type=F32) * inverse
            stores.append((mixed_t, at[0], out))
        if dmixed_t is not None:
            weights = raised * inverse
            d_out = d_mixed.astype(BF16)
            d_weights = lax.dot_general(v_low, d_out, TN, preferred_element_type=F32)
            shift = jnp.sum(weights * d_weights, axis=0, keepdims=True)
            d_scores = (weights * (d_weights - shift)).astype(BF16)
            dv = jnp.dot(weights.astype(BF16), d_out.T, preferred_element_type=F32).T
            dq = jnp.dot(k_high.astype(BF16), d_scores, preferred_element_type=F32)
            dk = jnp.dot(d_scores, q_high.astype(BF16).T, preferred_element_type=F32).T
            dq = dq * (q_gain * root)
            dk = dk * k_gain
            stores.append((qkv_t, at[0], q_scale * (dq - q_hat * jnp.mean(q_hat * dq, axis=0, keepdims=True))))
            stores.append((qkv_t, at[1], k_scale * (dk - k_hat * jnp.mean(k_hat * dk, axis=0, keepdims=True))))
            stores.append((qkv_t, at[2], dv))
        return lanes, stores

    def body(index, carry):
        taken = [one(index * 4 + i // 2, i % 2) for i in range(8)]
        for lanes, stores in [compute(*t) for t in taken]:
            for ref, rows, value in stores:
                ref[rows, lanes] = value
        return carry

    lax.fori_loop(first, last, body, 0, unroll=unroll)


def wide_rows(source, used, ref):
    ref[:, :used] = source[...].T.astype(BF16)
    ref[:, used:] = jnp.zeros((TOKENS, ref.shape[1] - used), BF16)


def add_projection(x, mixed, proj_t, adaln, put):
    def body(rows):
        projected = jnp.dot(mixed[rows, :HD], proj_t[...], preferred_element_type=F32)
        put(rows, x(rows) + adaln[2:3, :] * projected)

    row_loop(TOKENS, 256, body)


def pull_norm(x, cot, dqkv, weight_t, adaln, work, put):
    third = MODEL // 3
    for i in range(3):
        work[i * TOKENS:(i + 1) * TOKENS, :third] = jnp.dot(
            dqkv[:, :3 * HD], weight_t[:, i * third:(i + 1) * third], preferred_element_type=F32)

    def body(rows):
        d_normed = jnp.concatenate(
            [work[pl.ds(pl.multiple_of(i * TOKENS + rows.start, 8), rows.size), :third] for i in range(3)], axis=1)
        hat, scale = centred(x(rows))
        u = d_normed * (1.0 + adaln[1:2, :])
        d_x = scale * (u - jnp.mean(u, axis=-1, keepdims=True) - hat * jnp.mean(u * hat, axis=-1, keepdims=True))
        put(rows, cot(rows) + d_x)

    row_loop(TOKENS, 16, body, 4)


def gradient_part(left, right, first_tile, tiles, slab, work, beside=None):
    done = 0
    while done < tiles:
        size = min(2, tiles - done)
        lane = pl.multiple_of((first_tile + done) * 128, 128)
        out = jnp.dot(left[...], right[:, pl.ds(lane, size * 128)], preferred_element_type=F32)
        for t in range(size):
            work[(done + t) * MODEL:(done + t + 1) * MODEL, :] = out[:, t * 128:(t + 1) * 128]
        done += size
        if beside is not None:
            beside()

    pad = slab.shape[-2] - 8 * tiles - 8

    def gather(wide, carry):
        goal, base = slab.at[wide // 8, (wide // 2) % 4, wide % 2], pl.multiple_of(wide * 72, 8)
        for narrow in range(8):
            at = base + 9 * narrow
            rows = [work[pl.ds(t * MODEL + at, 8), :] for t in range(tiles)]
            rows.append(work[pl.ds(at + 8, 8, stride=MODEL), :])
            if pad:
                rows.append(jnp.zeros((pad, 128), F32))
            goal[narrow // 2, narrow % 2] = jnp.concatenate(rows, axis=0).astype(BF16)
        return carry

    lax.fori_loop(0, SHARDS // 8, gather, 0)


def split_pairs(pairs, tokens, beside):
    def body(rows):
        beside(rows.start // 16)
        for which in range(2):
            tokens[pl.ds(pl.multiple_of(which * SEQ + rows.start, 16), 16), :] = pairs[rows, which, :]

    row_loop(SEQ, 16, body)


def join_pairs(tokens, pairs):
    def body(rows):
        for which in range(2):
            pairs[rows, which, :] = tokens[pl.ds(pl.multiple_of(which * SEQ + rows.start, 16), 16), :]

    row_loop(SEQ, 16, body)


def pack_messages(source, send):
    top = lax.broadcasted_iota(jnp.int32, (8, 128), 0) < 2

    def body(s, carry):
        rows = [source[pl.ds(a * SEQ + 2 * s + b, 8, stride=TOKENS), :] for a in range(2) for b in range(2)]
        last = 8 * TOKENS + 2 * s
        rows.append(jnp.where(top, source[pl.ds(last, 8), :], source[pl.ds(last + SEQ - 2, 8), :]))
        send[s] = jnp.concatenate(rows, axis=0).astype(BF16)
        return carry

    lax.fori_loop(0, SHARDS, body, 0, unroll=4)


def unpack_messages(recv, target):
    def body(s, carry):
        rows = recv[s].astype(F32)
        for a in range(2):
            for b in range(2):
                at = (a * 2 + b) * 8
                target[pl.ds(b * SEQ + 2 * s + a, 8, stride=TOKENS), :] = rows[at:at + 8]
            target[pl.ds(8 * TOKENS + 2 * s + a, 2, stride=SEQ), :] = rows[32 + 2 * a:34 + 2 * a]
        return carry

    lax.fori_loop(0, SHARDS, body, 0, unroll=4)


class Exchange:
    def __init__(self, me, send, recv, send_sem, recv_sem, own_sem):
        self.me, self.send, self.recv, self.sems = me, send, recv, (send_sem, recv_sem)
        self.own = pltpu.make_async_copy(send.at[me], recv.at[me], own_sem)
        self.next = 1

    def one(self, step):
        other = (self.me + step * 37) % SHARDS
        pltpu.make_async_remote_copy(
            src_ref=self.send.at[other], dst_ref=self.recv.at[self.me], send_sem=self.sems[0], recv_sem=self.sems[1],
            device_id=(other // 8, other % 8), device_id_type=MESH).start()

    def some(self, count):
        first, self.next = self.next, min(self.next + count, SHARDS)
        lax.fori_loop(first, self.next, lambda step, c: (self.one(step), c)[1], 0)

    def every(self):
        other = (self.me + 1) % SHARDS
        return pltpu.make_async_remote_copy(
            src_ref=self.send.at[pl.ds(0, SHARDS - 1)], dst_ref=self.recv.at[pl.ds(0, SHARDS - 1)],
            send_sem=self.sems[0], recv_sem=self.sems[1], device_id=(other // 8, other % 8), device_id_type=MESH)

    def wait_recv(self):
        self.own.wait()
        self.every().wait_recv()

    def wait_send(self):
        self.every().wait_send()


def add_rows(count, target, sources):
    def step(index, carry):
        total = sources[0](index).astype(F32)
        for source in sources[1:]:
            total = total + source(index).astype(F32)
        target(index, total.astype(BF16))
        return carry

    lax.fori_loop(0, count, step, 0)


class Scatter:
    def __init__(self, at, slabs, buffers, sems, base, sums, which, scale):
        self.at, self.slabs, self.sums, self.which, self.scale = at, slabs, sums, which, scale
        self.from_core, self.first, self.second, self.third, *recvs = [
            buffers[i * COUNT:(i + 1) * COUNT] for i in range(7)]
        self.bufs, self.recvs = (self.first, self.second, self.third), recvs
        self.send_sem, self.recv_sem = sems
        self.base = base
        self.core, self.flying = {}, {}

    def copy(self, key, slot, src, dst, axis, step):
        slot = self.base + slot
        made = pltpu.make_async_remote_copy(
            src_ref=src, dst_ref=dst, send_sem=self.send_sem.at[slot], recv_sem=self.recv_sem.at[slot],
            device_id=device_of(moved(self.at, axis, step)), device_id_type=MESH)
        made.start()
        self.flying[key] = made

    def begin(self, part):
        self.copy((part, "core"), COUNT * 18 + part, self.slabs[part].at[:, :, 1 - self.at["core"]],
                  self.from_core[part], "core", 1)

    def join_cores(self, part):
        self.flying[(part, "core")].wait_recv()
        order, first = PARTS[part][3], self.first[part]
        mine, theirs, core = self.slabs[part], self.from_core[part], self.at["core"]

        def target(i, value):
            digit = {"x": (i % 2) * 2 + i // 32, "y": (i // 8) % 4, "z": (i // 2) % 4}
            first[digit[order[0]], digit[order[1]], digit[order[2]]] = value

        add_rows(64, target, [lambda i: mine[i // 32, (i // 8) % 4, core, (i // 2) % 4, i % 2],
                              lambda i: theirs[i // 32, (i // 8) % 4, (i // 2) % 4, i % 2]])
        self.start(part, 0)

    @staticmethod
    def halves(level, block):
        cut = 2 if level < 2 else 32
        return block.at[0:cut], block.at[cut:block.shape[0]]

    def start(self, part, level):
        axis = PARTS[part][3][level]
        here, source, recv = self.at[axis], self.bufs[level][part], self.recvs[level][part]
        for direction in (0, 1):
            step = 3 if direction else 1
            relay, plain = direction, 1 - direction
            far, near = source.at[(here + 2) % 4], source.at[(here + step) % 4]
            slot = ((part * 3 + level) * 2 + direction) * 3
            self.copy((part, level, direction, 0), slot, self.halves(level, far)[relay],
                      self.halves(level, recv.at[direction, 0])[relay], axis, step)
            self.copy((part, level, direction, 1), slot + 1, self.halves(level, near)[plain],
                      self.halves(level, recv.at[direction, 1])[plain], axis, step)

    def relay(self, part, level):
        axis = PARTS[part][3][level]
        here, source, recv = self.at[axis], self.bufs[level][part], self.recvs[level][part]
        for direction in (0, 1):
            step = 3 if direction else 1
            self.flying[(part, level, direction, 0)].wait_recv()
            near = self.halves(level, source.at[(here + step) % 4])[direction]
            came = self.halves(level, recv.at[direction, 0])[direction]
            if level == 0:
                def target(i, v):
                    came[i // 4, i % 4] = v
                add_rows(8, target, [lambda i: came[i // 4, i % 4], lambda i: near[i // 4, i % 4]])
            elif level == 1:
                def target(i, v):
                    came[i] = v
                add_rows(2, target, [lambda i: came[i], lambda i: near[i]])
            else:
                came[...] = (came[...].astype(F32) + near[...].astype(F32)).astype(BF16)
            slot = ((part * 3 + level) * 2 + direction) * 3 + 2
            self.copy((part, level, direction, 2), slot, came, self.halves(level, recv.at[direction, 1])[direction],
                      axis, step)

    def finish(self, part, level):
        axis = PARTS[part][3][level]
        source, recv = self.bufs[level][part].at[self.at[axis]], self.recvs[level][part]
        for direction in (0, 1):
            self.flying[(part, level, direction, 1)].wait_recv()
            self.flying[(part, level, direction, 2)].wait_recv()
        plus, minus = recv.at[0, 1], recv.at[1, 1]
        if level == 0:
            goal = self.second[part]

            def target(i, v):
                goal[i // 4, i % 4] = v
            add_rows(16, target, [lambda i: source[i // 4, i % 4], lambda i: plus[i // 4, i % 4],
                                  lambda i: minus[i // 4, i % 4]])
        elif level == 1:
            goal = self.third[part]

            def target(i, v):
                goal[i] = v
            add_rows(4, target, [lambda i: source[i], lambda i: plus[i], lambda i: minus[i]])
        else:
            start = sum(p[2] for p in PARTS[:part])
            self.sums[self.which, start:start + PARTS[part][2], :] = (
                source[...].astype(F32) + plus[...].astype(F32) + minus[...].astype(F32)) * self.scale

    def drain_cores(self):
        for part in range(COUNT):
            self.flying.pop((part, "core")).wait_send()

    def release(self, level, neighbours, free):
        for part in range(COUNT):
            for direction in (0, 1):
                for kind in range(3):
                    self.flying.pop((part, level, direction, kind)).wait_send()
        for peer in neighbours:
            pl.semaphore_signal(free.at[level], inc=1, device_id=peer, device_id_type=MESH)

    def drain(self):
        for made in self.flying.values():
            made.wait_send()


def parts_step(step, *level):
    for part in range(COUNT):
        step(part, *level)


def next_level(scatter, level):
    for part in range(COUNT):
        scatter.finish(part, level)
        scatter.start(part, level + 1)


def both_blocks(scale, clip_hbm, cot_hbm, wt_s_hbm, pt_s_hbm, adaln_s, gains_s, wt_t_hbm, pt_t_hbm, adaln_t, gains_t,
                result, grad_clip, sums,
                clip, pairs, cot, wt_s, pt_s, wt_t, pt_t, normed_s, normed_t, branch, qkv_s, qkv_t, mixed_f, dmixed_f,
                mixed_s, mixed_t, dqkv, left, work, tokens_b, send, recv_a, recv_b, slab0, slab1, slab2,
                *rest):
    buffers = rest[:7 * COUNT]
    load_sem, own_sem, send_a, send_b, got_a, got_b, sum_send, sum_recv, free_sem, core_free = rest[7 * COUNT:]
    at = place()
    me = lax.axis_index("wide") * 8 + lax.axis_index("narrow")
    loads = []
    for i, (hbm, vmem) in enumerate(((clip_hbm, clip), (wt_s_hbm, wt_s), (pt_s_hbm, pt_s), (cot_hbm, pairs),
                                     (pt_t_hbm, pt_t), (wt_t_hbm, wt_t))):
        load = pltpu.make_async_copy(hbm, vmem, load_sem.at[i])
        load.start()
        loads.append(load)
    barrier = pltpu.get_barrier_semaphore()

    def greet(step, carry):
        other = (me + step) % SHARDS
        pl.semaphore_signal(barrier, inc=1, device_id=(other // 8, other % 8), device_id_type=MESH)
        return carry

    lax.fori_loop(1, SHARDS, greet, 0)

    loads[0].wait()
    norm_tokens(flat_rows(clip), adaln_s, normed_s)
    loads[1].wait()
    project_qkv(wt_s, normed_s, qkv_s)
    heads_loop(qkv_s, gains_s, mixed_f, None)
    wide_rows(mixed_f, HD, mixed_s)
    loads[2].wait()
    add_projection(flat_rows(clip), mixed_s, pt_s, adaln_s, functools.partial(put_tiles, work))
    pack_messages(work, send)
    pl.semaphore_wait(barrier, SHARDS - 1)
    first = Exchange(me, send, recv_a, send_a, got_a, own_sem.at[0])
    first.own.start()
    first.some(8)

    def seven(index):
        for i in range(7):
            first.one(9 + index * 7 + i)


    loads[3].wait()
    split_pairs(pairs, cot, seven)
    first.next = 121
    first.some(7)
    gate_cotangent(flat_rows(cot), adaln_t, branch)
    loads[4].wait()
    pull_mixed(pt_t, branch, dmixed_f)
    loads[5].wait()
    first.wait_recv()
    unpack_messages(recv_a, tokens_b)
    middle = tile_rows(tokens_b)
    norm_tokens(middle, adaln_t, normed_t)
    project_qkv(wt_t, normed_t, qkv_t)
    heads_loop(qkv_t, gains_t, mixed_f, dmixed_f)
    wide_rows(qkv_t, 3 * HD, dqkv)
    pull_norm(middle, flat_rows(cot), dqkv, wt_t, adaln_t, qkv_t, functools.partial(put_tiles, work))
    first.wait_send()
    pack_messages(work, send)
    second = Exchange(me, send, recv_b, send_b, got_b, own_sem.at[1])
    second.own.start()
    second.some(12)
    wide_rows(mixed_f, HD, mixed_t)

    def put_result(rows, value):
        normed_t[rows, :] = value.astype(BF16)

    slabs = (slab0, slab1, slab2)
    sems = (sum_send, sum_recv)
    partner = device_of(moved(at, "core", 1))
    neighbours = [device_of(moved(at, a, d)) for a in ("x", "y", "z") for d in (1, 3)]
    sum_t = Scatter(at, slabs, buffers, sems, 0, sums, 1, scale)
    sum_s = Scatter(at, slabs, buffers, sems, COUNT * 19, sums, 0, scale)
    left[...] = normed_t[...].T
    for part in (0, 1):
        gradient_part(left, dqkv, PARTS[part][0], PARTS[part][1], slabs[part], work, lambda: second.some(11))
        sum_t.begin(part)
    left[...] = branch[...].T
    gradient_part(left, mixed_t, 0, PROJ_TILES, slabs[2], work, lambda: second.some(9))
    second.some(SHARDS)
    sum_t.begin(2)
    add_projection(middle, mixed_t, pt_t, adaln_t, put_result)
    join_pairs(normed_t, pairs)
    store_result = pltpu.make_async_copy(pairs, result, load_sem.at[6])
    store_result.start()

    second.wait_recv()
    parts_step(sum_t.join_cores)
    pl.semaphore_signal(core_free, inc=1, device_id=partner, device_id_type=MESH)
    unpack_messages(recv_b, tokens_b)
    d_middle = tile_rows(tokens_b)
    gate_cotangent(d_middle, adaln_s, branch)
    pull_mixed(pt_s, branch, dmixed_f)
    left[...] = branch[...].T
    sum_t.drain_cores()
    pl.semaphore_wait(core_free, 1)
    gradient_part(left, mixed_s, 0, PROJ_TILES, slabs[2], work)
    sum_s.begin(2)
    parts_step(sum_t.relay, 0)
    heads_loop(qkv_s, gains_s, None, dmixed_f)
    next_level(sum_t, 0)
    sum_t.release(0, neighbours, free_sem)

    def put_grad(rows, value):
        branch[rows, :] = value.astype(BF16)

    wide_rows(qkv_s, 3 * HD, dqkv)
    left[...] = normed_s[...].T
    gradient_part(left, dqkv, PARTS[0][0], PARTS[0][1], slabs[0], work)
    sum_s.begin(0)
    parts_step(sum_t.relay, 1)
    gradient_part(left, dqkv, PARTS[1][0], PARTS[1][1], slabs[1], work)
    sum_s.begin(1)
    pl.semaphore_wait(free_sem.at[0], len(neighbours))
    for part in (2, 0, 1):
        sum_s.join_cores(part)
    next_level(sum_t, 1)
    sum_t.release(1, neighbours, free_sem)
    pull_norm(flat_rows(clip), d_middle, dqkv, wt_s, adaln_s, qkv_s, put_grad)
    store_grad = pltpu.make_async_copy(branch, grad_clip, load_sem.at[7])
    store_grad.start()
    parts_step(sum_t.relay, 2)
    parts_step(sum_s.relay, 0)
    parts_step(sum_t.finish, 2)
    sum_t.release(2, neighbours, free_sem)
    pl.semaphore_wait(free_sem.at[1], len(neighbours))
    next_level(sum_s, 0)
    parts_step(sum_s.relay, 1)
    pl.semaphore_wait(free_sem.at[2], len(neighbours))
    next_level(sum_s, 1)
    parts_step(sum_s.relay, 2)
    parts_step(sum_s.finish, 2)
    sum_s.drain()
    second.wait_send()
    store_result.wait()
    store_grad.wait()


def split_sums(sums, result, grad_clip, qkv_s, proj_s, qkv_t, proj_t, result_out, grad_out, pairs, tokens, sems):
    taken = [pltpu.make_async_copy(result, pairs, sems.at[0]), pltpu.make_async_copy(grad_clip, tokens, sems.at[1])]
    given = [pltpu.make_async_copy(pairs, result_out, sems.at[2]), pltpu.make_async_copy(tokens, grad_out, sems.at[3])]
    for copy in taken:
        copy.start()
    for come, go in zip(taken, given):
        come.wait()
        go.start()
    for which, outs in enumerate(((qkv_s, proj_s), (qkv_t, proj_t))):
        start = 0
        for first, tiles, rows, _ in PARTS:
            out, base = (outs[0], 0) if first < QKV_TILES else (outs[1], QKV_TILES)
            for t in range(tiles):
                lane = (first + t - base) * 128
                width = min(128, out.shape[1] - lane)
                out[0:8, lane:lane + width] = sums[which, start + 8 * t:start + 8 * t + 8, :width]
                ninth = start + 8 * tiles + t
                out[8:9, lane:lane + width] = sums[which, ninth:ninth + 1, :width]
            start += rows
    for copy in given:
        copy.wait()


def run_blocks(scale, clip, cot, wt_s, pt_s, adaln_s, gains_s, wt_t, pt_t, adaln_t, gains_t):
    token, qkv_f, heads_f = ((TOKENS, MODEL), BF16), ((3 * HD, TOKENS), F32), ((HD, TOKENS), F32)
    tiles = ((LANE_TILES * TOKENS, 128), F32)
    mixed, message = ((TOKENS, PROJ_TILES * 128), BF16), ((SHARDS, MESSAGE, 128), BF16)
    pairs = ((SEQ, 2, MODEL), BF16)
    shapes = [token, pairs, token, ((3 * HD, MODEL), BF16), ((HD, MODEL), BF16), ((3 * HD, MODEL), BF16), ((HD, MODEL), BF16),
              token, token, token, qkv_f, qkv_f, heads_f, heads_f, mixed, mixed, ((TOKENS, QKV_TILES * 128), BF16),
              ((MODEL, TOKENS), BF16), ((8 * MODEL, 128), F32), tiles, message, message, message]
    shapes += [((2, 4, 2, 4, 2, rows, 128), BF16) for _, _, rows, _ in PARTS]
    for lead in ((2, 4, 4, 2), (4, 4, 4), (4, 4), (4,), (2, 2, 4, 4), (2, 2, 4), (2, 2)):
        shapes += [(lead + (rows, 128), BF16) for _, _, rows, _ in PARTS]
    vmem, hbm = pl.BlockSpec(memory_space=pltpu.VMEM), pl.BlockSpec(memory_space=pl.ANY)
    return pl.pallas_call(
        functools.partial(both_blocks, scale),
        out_shape=[jax.ShapeDtypeStruct(*pairs), jax.ShapeDtypeStruct(*token), jax.ShapeDtypeStruct((2, 176, 128), F32)],
        in_specs=[hbm, hbm, hbm, hbm, vmem, vmem, hbm, hbm, vmem, vmem],
        out_specs=[hbm, hbm, vmem],
        scratch_shapes=[pltpu.VMEM(*s) for s in shapes] + [
            pltpu.SemaphoreType.DMA((8,)), pltpu.SemaphoreType.DMA((2,)),
            pltpu.SemaphoreType.DMA, pltpu.SemaphoreType.DMA, pltpu.SemaphoreType.DMA, pltpu.SemaphoreType.DMA,
            pltpu.SemaphoreType.DMA((2 * COUNT * 19,)), pltpu.SemaphoreType.DMA((2 * COUNT * 19,)),
            pltpu.SemaphoreType.REGULAR((3,)), pltpu.SemaphoreType.REGULAR],
        compiler_params=pltpu.CompilerParams(collective_id=0, has_side_effects=True, vmem_limit_bytes=67043328),
        name="both_blocks",
    )(clip, cot, wt_s, pt_s, adaln_s, gains_s, wt_t, pt_t, adaln_t, gains_t)


def body(clip_tokens, cotangent, qkv_spatial, proj_spatial, adaln_spatial, qknorm_spatial,
         qkv_temporal, proj_temporal, adaln_temporal, qknorm_temporal):
    clip = clip_tokens.reshape(TOKENS, MODEL)
    result, grad_clip, sums = run_blocks(
        1.0 / math.sqrt(SEQ * SEQ), clip, cotangent, qkv_spatial.T, proj_spatial.T, adaln_spatial, qknorm_spatial,
        qkv_temporal.T, proj_temporal.T, adaln_temporal, qknorm_temporal)
    token, pairs = ((TOKENS, MODEL), BF16), ((SEQ, 2, MODEL), BF16)
    vmem, hbm = pl.BlockSpec(memory_space=pltpu.VMEM), pl.BlockSpec(memory_space=pl.ANY)
    *grads, result, grad_clip = pl.pallas_call(
        split_sums,
        out_shape=[jax.ShapeDtypeStruct((9, 3 * HD), F32), jax.ShapeDtypeStruct((9, HD), F32)] * 2 + [
            jax.ShapeDtypeStruct(*pairs), jax.ShapeDtypeStruct(*token)],
        in_specs=[vmem, hbm, hbm],
        out_specs=[vmem] * 4 + [hbm] * 2,
        scratch_shapes=[pltpu.VMEM(*pairs), pltpu.VMEM(*token), pltpu.SemaphoreType.DMA((4,))],
        name="split_sums",
    )(sums, result, grad_clip)
    return (result, grad_clip.reshape(2, SEQ, MODEL), *grads)


def solution(mesh):
    in_specs = (
        P(("wide", "narrow"), None, None),
        P(None, ("wide", "narrow"), None),
        P(),
        P(),
        P(),
        P(),
        P(),
        P(),
        P(),
        P(),
    )
    out_specs = (
        P(None, ("wide", "narrow"), None),
        P(("wide", "narrow"), None, None),
        P(("wide", "narrow"), None),
        P(("wide", "narrow"), None),
        P(("wide", "narrow"), None),
        P(("wide", "narrow"), None),
    )
    return jax.shard_map(body, mesh=mesh, in_specs=in_specs, out_specs=out_specs, check_vma=False)
```
